128 devices in a mesh: dp: 8 (over x, core), tensor: 16 (over z, y).
Axes of the slice: x: 4, y: 4, z: 4, core: 2. Of those that a mesh axis runs over, the one named last changes fastest.
Arguments:
- hidden_in: bfloat16 [16384, 4096], P(('dp', 'tensor')), parts along dimension 0, may hold values from -6 to 6
- norm_gain: bfloat16 [4096], replicated, may hold values from 0.099609375 to 1.8984375
- w_query: bfloat16 [4096, 4096], P(None, 'tensor'), may hold values from -0.09375 to 0.09375
- keyvalue_weight: bfloat16 [4096, 2048], P(None, 'tensor'), may hold values from -0.09375 to 0.09375
- w_out: bfloat16 [4096, 4096], P('tensor'), may hold values from -0.09375 to 0.09375
- prefix_keyvalue_cache: bfloat16 [4096, 2048], P(None, 'tensor'), may hold values from -600 to 600, as said below
- seg_ids: int32 [16384], P('dp'), parts along dimension 0, may hold values from 0 to 127, never falling along the last dimension, each value on 1 to 64 neighbouring positions
- seg_doc: int32 [1024], P('dp'), parts along dimension 0, may hold values from 0 to 15
- doc_lens: int32 [16], replicated, may hold values from 1 to 1024, 4096 in all
Outputs:
- mixed: bfloat16 [16384, 4096], P(('dp', 'tensor')), parts along dimension 0
The draws below stay inside these ranges and needn't reach their ends.
There are 8 independent parts, one for each index of `dp`. The reference program is written for one: setup_inputs(seed, part) draws one part's arguments, and reference() takes and returns one part's arrays. A program takes and returns all parts, laid end to end along the dimension named above; an argument that names none is the same for every part. Nothing has to cross between parts.
Inputs may be any that keep to these rules, and one draw needn't show every extreme that they name: `seg_ids`: segment numbers never fall along the tokens; each of the 128 samples holds 1 to 64 tokens, one exactly 64. `doc_lens`: the documents fill the prefix end to end in order, lengths summing to 4096, the longest exactly 1024. `prefix_keyvalue_cache`: cached keys already carry the rotary map of their prefix positions.
All inputs are finite; a program needn't handle non-finite values.
Results may differ from the reference program's by a relative error of at most 0.028.
The reference program's roundings to bfloat16 on the way count: a program that leaves them out, or rounds other values in their place, can miss the bound.
Values may be sent and summed in bfloat16 or wider, within the bound.
A program may use at most 192 MiB of HBM per device.

```python
import math
import jax
import jax.numpy as jnp
import numpy as np
from jax import lax

MODEL_WIDTH = 4096
QUERY_HEADS = 32
KEYVALUE_HEADS = 8
HEAD_SIZE = 128
PREFIX_SPAN = 4096
NDOCS = 16
SEG_MOST = 64
BATCH_TOKENS = 2048
SEGS = 128
DOC_MOST = 1024
N_TENSOR = 16


def draw_prefix_keyvalue_cache(key, part):
    column_span = KEYVALUE_HEADS * 2 * HEAD_SIZE
    base = jnp.clip(jax.random.normal(key, (PREFIX_SPAN, column_span), jnp.float32), -6.0, 6.0)
    return base.astype(jnp.bfloat16)


def with_ends(drawn, own_key, low, largest):
    place = [jax.random.randint(jax.random.fold_in(own_key, axis), (), 0, length) for axis, length in enumerate(drawn.shape)]
    widest = drawn.shape.index(max(drawn.shape))
    beside = place[:widest] + [(place[widest] + 1) % drawn.shape[widest]] + place[widest + 1:]
    return drawn.at[tuple(place)].set(low).at[tuple(beside)].set(largest)


def block_scale(stream_key, shape, pieces, smallest, top_value):
    factor_of, own = 1.0, jax.random.fold_in(stream_key, 6)
    for axis_at, blocks in pieces:
        draws = jnp.exp(jax.random.uniform(jax.random.fold_in(own, axis_at), (blocks,), jnp.float32, smallest / len(pieces), top_value / len(pieces)))
        factor_of = factor_of * jnp.repeat(draws, shape[axis_at] // blocks).reshape([-1 if axis == axis_at else 1 for axis in range(len(shape))])
    return factor_of


def split_up(number_of, total, reach, slope):
    portions = [(1 << 20) // math.isqrt(grade ** slope) + 1 for grade in range(2, number_of + 1)]
    surplus, given = total - reach - (number_of - 1), [1] * (number_of - 1)
    while surplus > 0:
        candidates = [i for i in range(number_of - 1) if given[i] < reach]
        pool, left = sum([portions[i] for i in candidates]), surplus
        for i in candidates:
            more = min(reach - given[i], max(1, left * portions[i] // pool), surplus)
            given[i] = given[i] + more
            surplus = surplus - more
    return np.array([reach] + given)


def uneven_parts(key, amount, total, limit, lean):
    if amount == 2:
        one = jax.random.randint(key, (), max(1, total - limit), min(limit, total - 1) + 1)
        return jnp.stack([one, total - one])
    sizes = jnp.asarray(split_up(amount, total, limit, lean), jnp.int32)
    twos = (amount - 1) // 2
    giver, sink = sizes[1:1 + 2 * twos:2], sizes[2:2 + 2 * twos:2]
    slack = jnp.minimum(giver - 1, limit - sink)
    passed = jax.random.randint(jax.random.fold_in(key, 1), (twos,), 0, 1 << 20) % (slack + 1)
    sizes = sizes.at[1:1 + 2 * twos:2].set(giver - passed).at[2:2 + 2 * twos:2].set(sink + passed)
    return sizes[jax.random.permutation(jax.random.fold_in(key, 2), amount)]


def normal_values(key, dims, spread, limit, shards=(), kind=jnp.bfloat16):
    level = block_scale(key, dims, shards, -0.22, 0.18) if shards else 1.0
    result = jax.random.normal(key, dims, jnp.float32) * spread * level
    return jnp.minimum(jnp.maximum(result, -limit), limit).astype(kind)


def setup_inputs(seed: int = 0, part: int = 0) -> dict:
    seeds = jax.random.split(jax.random.key(seed), 10)
    part_splits = jax.random.split(jax.random.fold_in(seeds[9], part), 10)
    hidden_in = normal_values(part_splits[0], (BATCH_TOKENS, MODEL_WIDTH), 1.0, 6.0, ((0, 16),))
    norm_gain = jnp.clip(1.0 + 0.18 * jax.random.normal(seeds[1], (MODEL_WIDTH,), jnp.float32), 0.099609375, 1.8984375).astype(jnp.bfloat16)
    w_query = normal_values(seeds[2], (MODEL_WIDTH, QUERY_HEADS * HEAD_SIZE), MODEL_WIDTH ** -0.5, 0.09375, ((1, 16),))
    keyvalue_weight = normal_values(seeds[3], (MODEL_WIDTH, KEYVALUE_HEADS * 2 * HEAD_SIZE), MODEL_WIDTH ** -0.5, 0.09375, ((1, 16),))
    w_out = normal_values(seeds[4], (QUERY_HEADS * HEAD_SIZE, MODEL_WIDTH), (QUERY_HEADS * HEAD_SIZE) ** -0.5, 0.09375, ((0, 16),))
    prefix_keyvalue_cache = draw_prefix_keyvalue_cache(jax.random.fold_in(seeds[9], 71), part)
    seg_ids = jnp.searchsorted(jnp.cumsum(uneven_parts(part_splits[6], SEGS, BATCH_TOKENS, SEG_MOST, 1)), jnp.arange(BATCH_TOKENS), side="right").astype(jnp.int32)
    seg_doc = with_ends(jax.random.randint(part_splits[7], (SEGS,), 0, NDOCS), jax.random.fold_in(part_splits[7], 1), 0, NDOCS - 1).astype(jnp.int32)
    doc_lens = uneven_parts(seeds[8], NDOCS, PREFIX_SPAN, DOC_MOST, 1).astype(jnp.int32)
    return {"hidden_in": hidden_in, "norm_gain": norm_gain, "w_query": w_query, "keyvalue_weight": keyvalue_weight, "w_out": w_out, "prefix_keyvalue_cache": prefix_keyvalue_cache, "seg_ids": seg_ids, "seg_doc": seg_doc, "doc_lens": doc_lens}


eps = 1e-05
rope_theta = 500000.0

def normalize(rows_in, gain):
    values = rows_in.astype(jnp.float32)
    mean_square = lax.optimization_barrier(jnp.mean(values * values, axis=-1, keepdims=True))
    return (values * lax.rsqrt(mean_square + eps) * gain.astype(jnp.float32)).astype(jnp.bfloat16)

def rotary_tables(positions, head_dim):
    half_dim = head_dim // 2
    inverse = rope_theta ** (-(jnp.arange(half_dim, dtype=jnp.float32) * 2.0 / head_dim))
    angles = positions.astype(jnp.float32)[:, None] * inverse[None, :]
    return (jnp.cos(angles), jnp.sin(angles))

def apply_rotation(vectors, cosine_table, sine_table):
    half_dim = vectors.shape[-1] // 2
    lower_half = vectors[..., :half_dim]
    upper_half = vectors[..., half_dim:]
    cos_part = cosine_table[:, None, :]
    sin_part = sine_table[:, None, :]
    return jnp.concatenate([lower_half * cos_part - upper_half * sin_part, upper_half * cos_part + lower_half * sin_part], axis=-1)

def token_tables(seg_ids, seg_doc, doc_lens, prefix_len):
    token_count = seg_ids.shape[0]
    token_order = jnp.arange(token_count, dtype=jnp.int32)
    seg_start = lax.optimization_barrier(jnp.sum((seg_ids[None, :] < seg_ids[:, None]).astype(jnp.int32), axis=1, dtype=jnp.int32))
    positions = prefix_len + token_order - seg_start
    segments = jnp.arange(seg_doc.shape[0], dtype=jnp.int32)
    tok_doc = lax.optimization_barrier(jnp.sum(jnp.where(seg_ids[:, None] == segments[None, :], seg_doc[None, :], 0), axis=1, dtype=jnp.int32))
    doc_ends = jnp.cumsum(doc_lens, dtype=jnp.int32)
    prefix_order = jnp.arange(prefix_len, dtype=jnp.int32)
    key_doc = lax.optimization_barrier(jnp.sum((doc_ends[None, :] <= prefix_order[:, None]).astype(jnp.int32), axis=1, dtype=jnp.int32))
    return (positions, tok_doc, key_doc)

def attend_block(query_matrix, all_keys, all_values, allowed, score_scale):
    scores = jnp.einsum('bmgd,kmd->bmgk', query_matrix.astype(jnp.float32), all_keys.astype(jnp.float32)) * score_scale
    scores = jnp.where(allowed[:, None, None, :], scores, -1e+30)
    row_max = lax.optimization_barrier(jnp.max(scores, axis=-1, keepdims=True))
    weights = jnp.exp(scores - row_max)
    row_total = lax.optimization_barrier(jnp.sum(weights, axis=-1, keepdims=True))
    weights_bf = (weights / row_total).astype(jnp.bfloat16)
    return jnp.einsum('bmgk,kmd->bmgd', weights_bf.astype(jnp.float32), all_values.astype(jnp.float32)).astype(jnp.bfloat16)

def reference(hidden_in, norm_gain, w_query, keyvalue_weight, w_out, prefix_keyvalue_cache, seg_ids, seg_doc, doc_lens):
    normalized_input = normalize(hidden_in, norm_gain)
    positions, tok_doc, key_doc = token_tables(seg_ids, seg_doc, doc_lens, PREFIX_SPAN)
    cosine_table, sine_table = rotary_tables(positions, HEAD_SIZE)
    group_width = QUERY_HEADS // KEYVALUE_HEADS
    query_projected = jnp.dot(normalized_input, w_query, preferred_element_type=jnp.float32).reshape(BATCH_TOKENS, QUERY_HEADS, HEAD_SIZE)
    query_matrix = apply_rotation(query_projected, cosine_table, sine_table).astype(jnp.bfloat16).reshape(BATCH_TOKENS, KEYVALUE_HEADS, group_width, HEAD_SIZE)
    keyvalue_projected = jnp.dot(normalized_input, keyvalue_weight, preferred_element_type=jnp.float32).reshape(BATCH_TOKENS, KEYVALUE_HEADS, 2, HEAD_SIZE)
    keys_new = apply_rotation(keyvalue_projected[:, :, 0], cosine_table, sine_table).astype(jnp.bfloat16)
    values_new = keyvalue_projected[:, :, 1].astype(jnp.bfloat16)
    cache_divided = prefix_keyvalue_cache.reshape(PREFIX_SPAN, KEYVALUE_HEADS, 2, HEAD_SIZE)
    all_keys = jnp.concatenate([cache_divided[:, :, 0], keys_new], axis=0)
    all_values = jnp.concatenate([cache_divided[:, :, 1], values_new], axis=0)
    block_rows = min(64, BATCH_TOKENS)
    score_scale = 1.0 / math.sqrt(HEAD_SIZE)
    token_order = jnp.arange(BATCH_TOKENS, dtype=jnp.int32)

    def one_block(block_index):
        first_row = block_index * block_rows
        query_rows = lax.dynamic_slice_in_dim(query_matrix, first_row, block_rows, 0)
        row_docs = lax.dynamic_slice_in_dim(tok_doc, first_row, block_rows, 0)
        row_segs = lax.dynamic_slice_in_dim(seg_ids, first_row, block_rows, 0)
        places = first_row + jnp.arange(block_rows, dtype=jnp.int32)
        prefix_ok = key_doc[None, :] == row_docs[:, None]
        own_ok = (seg_ids[None, :] == row_segs[:, None]) & (token_order[None, :] <= places[:, None])
        allowed = jnp.concatenate([prefix_ok, own_ok], axis=1)
        return attend_block(query_rows, all_keys, all_values, allowed, score_scale)
    attended = lax.map(one_block, jnp.arange(BATCH_TOKENS // block_rows, dtype=jnp.int32)).reshape(BATCH_TOKENS, QUERY_HEADS * HEAD_SIZE)
    per_group = QUERY_HEADS * HEAD_SIZE // N_TENSOR

    def add_group(running, group_index):
        first_col = group_index * per_group
        term = jnp.dot(lax.dynamic_slice_in_dim(attended, first_col, per_group, 1), lax.dynamic_slice_in_dim(w_out, first_col, per_group, 0), preferred_element_type=jnp.float32)
        rounded = lax.optimization_barrier(term.astype(jnp.bfloat16))
        return (running + rounded.astype(jnp.float32), None)
    summed, unused = lax.scan(add_group, jnp.zeros((BATCH_TOKENS, MODEL_WIDTH), jnp.float32), jnp.arange(N_TENSOR, dtype=jnp.int32))
    return (hidden_in.astype(jnp.float32) + summed).astype(jnp.bfloat16)
```

```python
import functools
import math

import jax
import jax.numpy as jnp
from jax import lax
from jax.experimental import pallas as pl
from jax.experimental.pallas import tpu as pltpu
from jax.sharding import PartitionSpec as P

HEAD = 128
HALO = 64
SIDE = 4
EPS = 1e-05
THETA = 500000.0
MASKED = -1e30
MESH = pl.DeviceIdType.MESH
BF16 = jnp.bfloat16
F32 = jnp.float32


def place():
    dp, tensor = lax.axis_index("dp"), lax.axis_index("tensor")
    return dp // 2, dp % 2, tensor // SIDE, tensor % SIDE


def device(x, core, z, y):
    return (2 * (x % SIDE) + core, SIDE * (z % SIDE) + y % SIDE)


def greet(others):
    barrier = pltpu.get_barrier_semaphore()
    for other in others:
        pl.semaphore_signal(barrier, inc=1, device_id=other, device_id_type=MESH)
    pl.semaphore_wait(barrier, len(others))


def remote(src, dst, send, recv, other):
    return pltpu.make_async_remote_copy(
        src_ref=src, dst_ref=dst, send_sem=send, recv_sem=recv, device_id=other, device_id_type=MESH
    )


def rotate(v, cos, sin):
    return v * cos + pltpu.roll(v, HEAD // 2, 1) * sin


class Spread:
    def __init__(self, own, block, send, recv):
        self.own, self.block, self.send, self.recv = own, block, send, recv
        self.x, self.core, self.z, self.y = place()

    def number(self, parity, core, half):
        return 4 * parity + 2 * core + half

    def up(self, n):
        return (self.x, self.core, self.z, self.y + n)

    def copy(self, i, d, piece, to, first=False):
        slot = (self.y + d + SIDE) % SIDE
        src = self.own(piece) if first else self.block(slot, piece)
        return remote(
            src, self.block(slot, piece), self.send.at[i], self.recv.at[i], device(*to)
        )

    def mine(self, half):
        return self.number(self.x % 2, self.core, half)

    def sends(self, i):
        if i in (0, 1):
            return self.copy(i, 0, self.mine(i), self.up(1), True)
        if i == 2:
            return self.copy(i, 3, self.mine(0), self.up(1))
        if i in (3, 4):
            return self.copy(i, 0, self.mine(4 - i), self.up(SIDE - 1), True)
        if i == 5:
            return self.copy(i, 1, self.mine(1), self.up(SIDE - 1))
        d, half = 1 + (i % 6) // 2, i % 2
        if i < 12:
            to = (self.x + (SIDE - 1 if half else 1), self.core, self.z, self.y)
            return self.copy(i, d, self.mine(half), to)
        parity = self.x % 2 if i < 18 else 1 - self.x % 2
        piece = self.number(parity, self.core, half)
        return self.copy(i, d, piece, (self.x, 1 - self.core, self.z, self.y))

    def got(self, i):
        if i < 6:
            d = {0: 3, 1: 3, 2: 2, 3: 1, 4: 1, 5: 2}[i]
            half = {0: 0, 1: 1, 2: 0, 3: 1, 4: 0, 5: 1}[i]
            piece = self.mine(half)
        else:
            d, half = 1 + (i % 6) // 2, i % 2
            parity = self.x % 2 if 12 <= i < 18 else 1 - self.x % 2
            core = self.core if i < 12 else 1 - self.core
            piece = self.number(parity, core, half)
        view = self.block((self.y + d) % SIDE, piece)
        remote(view, view, self.send.at[i], self.recv.at[i], device(*self.up(1))).wait_recv()

    def start(self):
        for i in (0, 3, 1, 4):
            self.sends(i).start()

    def along_y(self, i):
        self.got(i)
        if i == 0:
            self.sends(2).start()
        if i == 3:
            self.sends(5).start()
        d = {0: 3, 1: 3, 2: 2, 3: 1, 4: 1, 5: 2}[i]
        half = {0: 0, 1: 1, 2: 0, 3: 1, 4: 0, 5: 1}[i]
        self.sends(6 + 2 * (d - 1) + half).start()
        self.sends(12 + 2 * (d - 1) + half).start()

    def along_x(self, i):
        self.got(i)
        self.sends(i + 12).start()

    def sibling(self):
        for i in range(12, 24):
            self.got(i)

    def sent(self):
        for i in range(24):
            self.sends(i).wait_send()


Y_ORDER = (0, 3, 1, 4, 2, 5)
X_ORDER = (10, 7, 11, 6, 8, 9)


def gather_project(
    hid, gain, cos, sin, wq, wkv, pfx, wo,
    q_out, kv, pfx_all, wo_all,
    xs, wqs, wkvs, send, recv, x_send, x_recv, halo_send, halo_recv, local,
):
    x, core, z, y = place()
    here = lambda dx, dcore, dz, dy: device(
        x + dx, core if dcore == 0 else 1 - core, z + dz, y + dy
    )
    down = SIDE - 1
    greet([
        here(0, 0, 0, 1), here(0, 0, 0, down), here(0, 0, 1, 0), here(0, 0, down, 0),
        here(1, 0, 0, 0), here(down, 0, 0, 0), here(0, 1, 0, 0),
    ])

    def rows(array, count):
        return lambda n: array.at[pl.ds(pl.multiple_of(n * count, count), count), :]

    def blocks(array, count):
        return lambda s, n: array.at[s, pl.ds(pl.multiple_of(n * count, count), count), :]

    spreads = [
        Spread(rows(own, count), blocks(every, count), send.at[k], recv.at[k])
        for k, (own, every, count) in enumerate(
            [(wkv, wkvs, 512), (wq, wqs, 512), (pfx, pfx_all, 512), (wo, wo_all, 32)]
        )
    ]
    skv, sq, sp, so = spreads
    skv.start()
    sq.start()

    values = hid[...].astype(F32)
    scale = lax.rsqrt(jnp.mean(values * values, axis=-1, keepdims=True) + EPS)
    xs[z] = (values * scale * gain[...].astype(F32)).astype(BF16)

    def x_send_copy(i):
        slot = {0: z, 1: z, 2: z + 3, 3: z, 4: z, 5: z + 1}[i] % SIDE
        half = {0: 0, 1: 1, 2: 0, 3: 1, 4: 0, 5: 1}[i]
        to = here(0, 0, 1, 0) if i < 3 else here(0, 0, down, 0)
        view = xs.at[slot, pl.ds(64 * half, 64), :]
        return remote(view, view, x_send.at[i], x_recv.at[i], to)

    def x_got(i):
        slot = {0: z + 3, 1: z + 3, 2: z + 2, 3: z + 1, 4: z + 1, 5: z + 2}[i] % SIDE
        half = {0: 0, 1: 1, 2: 0, 3: 1, 4: 0, 5: 1}[i]
        view = xs.at[slot, pl.ds(64 * half, 64), :]
        remote(view, view, x_send.at[i], x_recv.at[i], here(0, 0, 1, 0)).wait_recv()

    for i in (0, 3, 1, 4):
        x_send_copy(i).start()
    stays = [
        pltpu.make_async_copy(own, every.at[y], local.at[k])
        for k, (own, every) in enumerate([(wkv, wkvs), (wq, wqs), (pfx, pfx_all), (wo, wo_all)])
    ]
    for copy in stays:
        copy.start()

    for i in (0, 3):
        skv.along_y(i)
    for i in (0, 3):
        x_got(i)
        x_send_copy(i + 2).start()
    for i in (1, 4, 2, 5):
        skv.along_y(i)
    for i in (0, 3):
        sq.along_y(i)
    for i in X_ORDER:
        skv.along_x(i)
    sp.start()
    for i in (1, 4, 2, 5):
        sq.along_y(i)
    for i in (0, 3):
        sp.along_y(i)
    for i in X_ORDER:
        sq.along_x(i)
    so.start()
    for i in (1, 4, 2, 5):
        x_got(i)
    skv.sibling()
    sq.sibling()
    stays[0].wait()
    stays[1].wait()

    half_rows = 2 * 128

    def project_kv():
        for s in range(SIDE):
            @pl.loop(0, 2)
            def _(m):
                tall = pl.ds(pl.multiple_of(m * half_rows, half_rows), half_rows)
                lhs = xs[pl.ds(2 * m, 2)].reshape(half_rows, xs.shape[2])
                got = jnp.dot(lhs, wkvs[s], preferred_element_type=F32)
                if s % 2 == 0:
                    got = rotate(got, cos[tall, :], sin[tall, :])
                got = got.astype(BF16).reshape(2, 128, HEAD)
                kv[pl.ds(2 * m, 2), pl.ds(HALO, 128), pl.ds(HEAD * s, HEAD)] = got

    def project_q(s):
        @pl.loop(0, 2)
        def _(m):
            tall = pl.ds(pl.multiple_of(m * half_rows, half_rows), half_rows)
            lhs = xs[pl.ds(2 * m, 2)].reshape(half_rows, xs.shape[2])
            got = jnp.dot(lhs, wqs[s], preferred_element_type=F32)
            for n in range(2):
                one = rotate(got[:, HEAD * n : HEAD * (n + 1)], cos[tall, :], sin[tall, :])
                q_out[tall, pl.ds(HEAD * (2 * s + n), HEAD)] = one.astype(BF16)

    def halo_copy(slot):
        dst = (slot + y // 3) % SIDE
        return remote(
            kv.at[slot, pl.ds(128, HALO), :],
            kv.at[dst, pl.ds(0, HALO), :],
            halo_send.at[slot],
            halo_recv.at[slot],
            here(0, 0, 0, 1),
        )

    project_kv()
    for slot in range(SIDE):
        halo_copy(slot).start()
    for i in (1, 4, 2, 5):
        sp.along_y(i)
    project_q(0)
    for i in (0, 3):
        so.along_y(i)
    for i in X_ORDER[:4]:
        sp.along_x(i)
    project_q(1)
    for i in X_ORDER[4:]:
        sp.along_x(i)
    for i in (1, 4):
        so.along_y(i)
    project_q(2)
    for i in (2, 5):
        so.along_y(i)
    project_q(3)
    for i in X_ORDER:
        so.along_x(i)
    sp.sibling()
    so.sibling()
    stays[2].wait()
    stays[3].wait()
    for slot in range(SIDE):
        halo_copy(slot).wait()
    for i in range(6):
        x_send_copy(i).wait_send()
    for spread in spreads:
        spread.sent()


def attend(
    bounds, rank_row, rank_col, meta, key_doc, key_seg, key_pos, q, kv, pfx,
    out, perm, qs, ms, outs, top, total, acc,
):
    tokens = q.shape[0]
    order = lax.broadcasted_iota(jnp.int32, (tokens, tokens), 0)
    perm[...] = (rank_row[...] == order).astype(F32).astype(BF16)
    qs[...] = jnp.dot(perm[...], q[...], preferred_element_type=F32).astype(BF16)
    ms[...] = jnp.dot(perm[...], meta[...], preferred_element_type=F32)
    tile, keys, group = 128, 256, 4
    score_scale = 1.0 / math.sqrt(HEAD)

    @pl.loop(0, tokens // tile)
    def _(i):
        rows = pl.ds(pl.multiple_of(i * tile, tile), tile)
        top[...] = jnp.full(top.shape, MASKED, F32)
        total[...] = jnp.zeros(total.shape, F32)
        acc[...] = jnp.zeros(acc.shape, F32)
        queries = [
            jnp.concatenate(
                [qs[rows, pl.ds(HEAD * (group * h + n), HEAD)] for n in range(group)], axis=0
            )
            for h in range(2)
        ]

        def step(key, value, allowed):
            bias = jnp.where(allowed, 0.0, MASKED)
            for h in range(2):
                s = lax.dot_general(
                    queries[h], key[h], (((1,), (1,)), ((), ())), preferred_element_type=F32
                )
                s = s * score_scale
                s = jnp.where(
                    jnp.broadcast_to((bias < 0.0)[None], (group, tile, keys)),
                    MASKED,
                    s.reshape(group, tile, keys),
                ).reshape(group * tile, keys)
                old = top[h, :, :1]
                new = jnp.maximum(old, jnp.max(s, axis=-1, keepdims=True))
                p = jnp.exp(s - new)
                fade = jnp.exp(old - new)
                top[h] = jnp.broadcast_to(new, top.shape[1:])
                total[h] = total[h] * fade + jnp.sum(p, axis=-1, keepdims=True)
                acc[h] = acc[h] * fade + jnp.dot(
                    p.astype(BF16), value[h], preferred_element_type=F32
                )

        seg, pos, doc = ms[rows, 1:2], ms[rows, 2:3], ms[rows, 0:1]

        @pl.loop(0, kv.shape[0] // keys)
        def _(j):
            cut = pl.ds(pl.multiple_of(j * keys, keys), keys)
            allowed = (key_seg[j] == seg) & (key_pos[j] <= pos)
            step(
                [kv[cut, pl.ds(2 * HEAD * h, HEAD)] for h in range(2)],
                [kv[cut, pl.ds(2 * HEAD * h + HEAD, HEAD)] for h in range(2)],
                allowed,
            )

        @pl.loop(bounds[i], bounds[SIDE + i])
        def _(j):
            cut = pl.ds(pl.multiple_of(j * keys, keys), keys)
            allowed = key_doc[j] == doc
            step(
                [pfx[2 * h, cut, :] for h in range(2)],
                [pfx[2 * h + 1, cut, :] for h in range(2)],
                allowed,
            )

        for h in range(2):
            done = (acc[h] / total[h]).astype(BF16)
            for n in range(group):
                outs[rows, pl.ds(HEAD * (group * h + n), HEAD)] = done[n * tile : (n + 1) * tile]

    order = lax.broadcasted_iota(jnp.int32, (tokens, tokens), 1)
    perm[...] = (rank_col[...] == order).astype(F32).astype(BF16)
    out[...] = jnp.dot(perm[...], outs[...], preferred_element_type=F32).astype(BF16)


COLS = 512


def project_reduce(
    att, wo, hid, mixed,
    far_out, near_out, far_in, near_in, far_send, far_recv, near_send, near_recv,
):
    x, core, z, y = place()
    sides = [device(x, core, z + 1, y), device(x, core, z + SIDE - 1, y)]
    greet(sides)
    chunks = wo.shape[1] // COLS

    def partial(slot, j):
        return jnp.dot(
            att[slot % SIDE], wo[:, pl.ds(COLS * j, COLS)], preferred_element_type=F32
        )

    def far(j):
        return remote(
            far_out.at[j], far_in.at[j], far_send.at[j], far_recv.at[j], sides[j % 2]
        )

    def near(side, j):
        return remote(
            near_out.at[side, j],
            near_in.at[side, j],
            near_send.at[side, j],
            near_recv.at[side, j],
            sides[side],
        )

    for j in range(chunks):
        far_out[j] = partial(z + 2, j).astype(BF16)
        far(j).start()
    for j in range(chunks):
        side = 1 - j % 2
        near_out[side, j] = partial(z + (3 if side else 1), j).astype(BF16)
        near(side, j).start()
        side = j % 2
        mine = partial(z + (3 if side else 1), j)
        far(j).wait_recv()
        near_out[side, j] = (mine + far_in[j].astype(F32)).astype(BF16)
        near(side, j).start()
    for j in range(chunks):
        cut = pl.ds(COLS * j, COLS)
        mine = partial(z, j) + hid[:, cut].astype(F32)
        near(0, j).wait_recv()
        near(1, j).wait_recv()
        mine = mine + near_in[0, j].astype(F32) + near_in[1, j].astype(F32)
        mixed[:, cut] = mine.astype(BF16)
    for j in range(chunks):
        far(j).wait_send()
        near(0, j).wait_send()
        near(1, j).wait_send()


def tables(seg_ids, seg_doc, doc_lens, prefix_len):
    y = lax.axis_index("tensor") % SIDE
    padded = jnp.concatenate([jnp.full((HALO,), -1, jnp.int32), seg_ids])
    span = HALO + 128
    starts = [128 * (SIDE * s + y) for s in range(SIDE)]
    key_seg = jnp.concatenate([lax.dynamic_slice_in_dim(padded, a, span) for a in starts])
    places = jnp.concatenate([a - HALO + jnp.arange(span, dtype=jnp.int32) for a in starts])
    before = jnp.sum((seg_ids[None, :] < key_seg[:, None]).astype(jnp.int32), axis=1)
    key_pos = places - before
    seg = key_seg.reshape(SIDE, span)[:, HALO:].reshape(-1)
    pos = key_pos.reshape(SIDE, span)[:, HALO:].reshape(-1)
    segments = jnp.arange(seg_doc.shape[0], dtype=jnp.int32)
    doc = jnp.sum(jnp.where(seg[:, None] == segments[None, :], seg_doc[None, :], 0), axis=1)
    docs = jnp.arange(doc_lens.shape[0], dtype=jnp.int32)
    ends = jnp.sum(jnp.where(docs[None, :] <= docs[:, None], doc_lens[None, :], 0), axis=1)
    at = jnp.arange(prefix_len, dtype=jnp.int32)
    key_doc = jnp.sum((ends[None, :] <= at[:, None]).astype(jnp.int32), axis=1)
    order = doc * seg.shape[0] + jnp.arange(seg.shape[0], dtype=jnp.int32)
    rank = jnp.sum((order[None, :] < order[:, None]).astype(jnp.int32), axis=1)
    upto = jnp.sum((doc[None, :] <= docs[:, None]).astype(jnp.int32), axis=1)
    tile = jnp.arange(SIDE, dtype=jnp.int32) * 128
    first = jnp.sum((upto[None, :] <= tile[:, None]).astype(jnp.int32), axis=1)
    last = jnp.sum((upto[None, :] <= tile[:, None] + 127).astype(jnp.int32), axis=1)
    low = jnp.sum(jnp.where(docs[None, :] < first[:, None], doc_lens[None, :], 0), axis=1)
    high = jnp.sum(jnp.where(docs[None, :] <= last[:, None], doc_lens[None, :], 0), axis=1)
    bounds = jnp.concatenate([low // 256, (high + 255) // 256])
    return key_seg, key_pos, seg, pos, doc, key_doc, rank, bounds


def local(hidden_in, norm_gain, w_query, keyvalue_weight, w_out, cache, seg_ids, seg_doc, doc_lens):
    prefix_len = cache.shape[0]
    width = hidden_in.shape[1]
    key_seg, key_pos, seg, pos, doc, key_doc, rank, bounds = tables(
        seg_ids, seg_doc, doc_lens, prefix_len
    )
    half = HEAD // 2
    inverse = THETA ** (-(jnp.arange(half, dtype=F32) * 2.0 / HEAD))
    angles = (prefix_len + pos).astype(F32)[:, None] * inverse[None, :]
    cos, sin = jnp.cos(angles), jnp.sin(angles)
    cos = jnp.concatenate([cos, cos], axis=1)
    sin = jnp.concatenate([-sin, sin], axis=1)

    vmem = pl.BlockSpec(memory_space=pltpu.VMEM)
    smem = pl.BlockSpec(memory_space=pltpu.SMEM)
    whole = pl.BlockSpec(memory_space=pl.ANY)
    tokens = SIDE * 128
    q, kv, pfx, wo = pl.pallas_call(
        gather_project,
        out_shape=(
            jax.ShapeDtypeStruct((tokens, 8 * HEAD), BF16),
            jax.ShapeDtypeStruct((SIDE, HALO + 128, 4 * HEAD), BF16),
            jax.ShapeDtypeStruct((SIDE, prefix_len, HEAD), BF16),
            jax.ShapeDtypeStruct((SIDE,) + w_out.shape, BF16),
        ),
        in_specs=[vmem] * 4 + [whole] * 4,
        out_specs=(vmem, vmem, whole, whole),
        scratch_shapes=[
            pltpu.VMEM((SIDE, 128, width), BF16),
            pltpu.VMEM((SIDE,) + w_query.shape, BF16),
            pltpu.VMEM((SIDE,) + keyvalue_weight.shape, BF16),
            pltpu.SemaphoreType.DMA((4, 24)),
            pltpu.SemaphoreType.DMA((4, 24)),
            pltpu.SemaphoreType.DMA((6,)),
            pltpu.SemaphoreType.DMA((6,)),
            pltpu.SemaphoreType.DMA((4,)),
            pltpu.SemaphoreType.DMA((4,)),
            pltpu.SemaphoreType.DMA((4,)),
        ],
        compiler_params=pltpu.CompilerParams(
            collective_id=0, has_side_effects=True, vmem_limit_bytes=48 * 2**20
        ),
        name="gather_project",
    )(hidden_in, norm_gain[None, :], cos, sin, w_query, keyvalue_weight, cache, w_out)

    meta = jnp.stack([doc, seg, pos], axis=1).astype(BF16)
    meta = jnp.pad(meta, ((0, 0), (0, HEAD - 3)))
    attended = pl.pallas_call(
        attend,
        out_shape=jax.ShapeDtypeStruct((tokens, 8 * HEAD), BF16),
        in_specs=[smem] + [vmem] * 9,
        out_specs=vmem,
        scratch_shapes=[
            pltpu.VMEM((tokens, tokens), BF16),
            pltpu.VMEM((tokens, 8 * HEAD), BF16),
            pltpu.VMEM((tokens, HEAD), F32),
            pltpu.VMEM((tokens, 8 * HEAD), BF16),
            pltpu.VMEM((2, tokens, HEAD), F32),
            pltpu.VMEM((2, tokens, HEAD), F32),
            pltpu.VMEM((2, tokens, HEAD), F32),
        ],
        compiler_params=pltpu.CompilerParams(vmem_limit_bytes=32 * 2**20),
        name="attend",
    )(
        bounds,
        rank[None, :],
        rank[:, None],
        meta,
        key_doc.astype(F32).reshape(-1, 1, 256),
        key_seg.astype(F32).reshape(-1, 1, 256),
        key_pos.astype(F32).reshape(-1, 1, 256),
        q,
        kv.reshape(SIDE * (HALO + 128), 4 * HEAD),
        pfx,
    )

    chunks = width // COLS
    return pl.pallas_call(
        project_reduce,
        out_shape=jax.ShapeDtypeStruct(hidden_in.shape, BF16),
        in_specs=[vmem] * 3,
        out_specs=vmem,
        scratch_shapes=[
            pltpu.VMEM((chunks, 128, COLS), BF16),
            pltpu.VMEM((2, chunks, 128, COLS), BF16),
            pltpu.VMEM((chunks, 128, COLS), BF16),
            pltpu.VMEM((2, chunks, 128, COLS), BF16),
            pltpu.SemaphoreType.DMA((chunks,)),
            pltpu.SemaphoreType.DMA((chunks,)),
            pltpu.SemaphoreType.DMA((2, chunks)),
            pltpu.SemaphoreType.DMA((2, chunks)),
        ],
        compiler_params=pltpu.CompilerParams(
            collective_id=1, has_side_effects=True, vmem_limit_bytes=32 * 2**20
        ),
        name="project_reduce",
    )(attended.reshape(SIDE, 128, 8 * HEAD), wo.reshape(-1, width), hidden_in)


def solution(mesh):
    return jax.shard_map(
        local,
        mesh=mesh,
        in_specs=(
            P(("dp", "tensor"), None),
            P(),
            P(None, "tensor"),
            P(None, "tensor"),
            P("tensor", None),
            P(None, "tensor"),
            P("dp"),
            P("dp"),
            P(),
        ),
        out_specs=P(("dp", "tensor"), None),
        check_vma=False,
    )
```

```python
import functools
import math

import jax
import jax.numpy as jnp
import numpy as np
from jax import lax
from jax.experimental import pallas as pl
from jax.experimental.pallas import tpu as pltpu
from jax.sharding import PartitionSpec as P

HEAD = 128
HALO = 64
SIDE = 4
EPS = 1e-05
THETA = 500000.0
MASKED = -1e30
MESH = pl.DeviceIdType.MESH
BF16 = jnp.bfloat16
F32 = jnp.float32


def place():
    dp, tensor = lax.axis_index("dp"), lax.axis_index("tensor")
    return dp // 2, dp % 2, tensor // SIDE, tensor % SIDE


def device(x, core, z, y):
    return (2 * (x % SIDE) + core, SIDE * (z % SIDE) + y % SIDE)


def greet(others):
    barrier = pltpu.get_barrier_semaphore()
    for other in others:
        pl.semaphore_signal(barrier, inc=1, device_id=other, device_id_type=MESH)
    pl.semaphore_wait(barrier, len(others))


def remote(src, dst, send, recv, other):
    return pltpu.make_async_remote_copy(
        src_ref=src, dst_ref=dst, send_sem=send, recv_sem=recv, device_id=other, device_id_type=MESH
    )


def rotate(v, cos, sin):
    return v * cos + pltpu.roll(v, HEAD // 2, 1) * sin


class Spread:
    def __init__(self, own, block, send, recv):
        self.own, self.block, self.send, self.recv = own, block, send, recv
        self.x, self.core, self.z, self.y = place()

    def number(self, parity, core, half):
        return 4 * parity + 2 * core + half

    def up(self, n):
        return (self.x, self.core, self.z, self.y + n)

    def copy(self, i, d, piece, to, first=False):
        slot = (self.y + d + SIDE) % SIDE
        src = self.own(piece) if first else self.block(slot, piece)
        return remote(
            src, self.block(slot, piece), self.send.at[i], self.recv.at[i], device(*to)
        )

    def mine(self, half):
        return self.number(self.x % 2, self.core, half)

    def sends(self, i):
        if i in (0, 1):
            return self.copy(i, 0, self.mine(i), self.up(1), True)
        if i == 2:
            return self.copy(i, 3, self.mine(0), self.up(1))
        if i in (3, 4):
            return self.copy(i, 0, self.mine(4 - i), self.up(SIDE - 1), True)
        if i == 5:
            return self.copy(i, 1, self.mine(1), self.up(SIDE - 1))
        d, half = 1 + (i % 6) // 2, i % 2
        if i < 12:
            to = (self.x + (SIDE - 1 if half else 1), self.core, self.z, self.y)
            return self.copy(i, d, self.mine(half), to)
        parity = self.x % 2 if i < 18 else 1 - self.x % 2
        piece = self.number(parity, self.core, half)
        return self.copy(i, d, piece, (self.x, 1 - self.core, self.z, self.y))

    def got(self, i):
        if i < 6:
            d = {0: 3, 1: 3, 2: 2, 3: 1, 4: 1, 5: 2}[i]
            half = {0: 0, 1: 1, 2: 0, 3: 1, 4: 0, 5: 1}[i]
            piece = self.mine(half)
        else:
            d, half = 1 + (i % 6) // 2, i % 2
            parity = self.x % 2 if 12 <= i < 18 else 1 - self.x % 2
            core = self.core if i < 12 else 1 - self.core
            piece = self.number(parity, core, half)
        view = self.block((self.y + d) % SIDE, piece)
        remote(view, view, self.send.at[i], self.recv.at[i], device(*self.up(1))).wait_recv()

    def start(self):
        for i in (0, 3, 1, 4):
            self.sends(i).start()

    def along_y(self, i):
        self.got(i)
        if i == 0:
            self.sends(2).start()
        if i == 3:
            self.sends(5).start()
        d = {0: 3, 1: 3, 2: 2, 3: 1, 4: 1, 5: 2}[i]
        half = {0: 0, 1: 1, 2: 0, 3: 1, 4: 0, 5: 1}[i]
        self.sends(6 + 2 * (d - 1) + half).start()
        self.sends(12 + 2 * (d - 1) + half).start()

    def along_x(self, i):
        self.got(i)
        self.sends(i + 12).start()

    def sibling(self):
        for i in range(12, 24):
            self.got(i)

    def sent(self):
        for i in range(24):
            self.sends(i).wait_send()


Y_ROUNDS = ((0, 3), (1, 4), (2, 5))
X_ROUNDS = ((10, 7), (11, 6), (8, 9))
PIECE = 16


def spread_rows(row):
    return jnp.transpose(jnp.broadcast_to(row, (128, row.shape[1])))


def count(flags):
    return jnp.sum(jnp.where(flags, 1.0, 0.0), axis=0, keepdims=True)


def describe(seg_ids, seg_doc, doc_lens, y):
    lane = lax.broadcasted_iota(jnp.int32, (1, 128), 1)

    def window(n):
        return seg_ids[:, pl.ds(pl.multiple_of(128 * jnp.maximum(n, 0), 128), 128)].astype(F32)

    own = [window(SIDE * s + y) for s in range(SIDE)]
    own_at = [(128 * (SIDE * s + y) + lane).astype(F32) for s in range(SIDE)]
    halo, halo_at = [], []
    for s in (0, 2):
        low, high = window(SIDE * s + y - 1), window(SIDE * (s + 1) + y - 1)
        both = jnp.where(lane < HALO, pltpu.roll(low, HALO, 1), high)
        start = jnp.where(
            lane < HALO, 128 * (SIDE * s + y) - HALO, 128 * (SIDE * (s + 1) + y) - 2 * HALO
        )
        at = (start + lane).astype(F32)
        halo.append(jnp.where(at < 0.0, -1.0, both))
        halo_at.append(at)
    seg = jnp.concatenate(own + halo, axis=1)
    at = jnp.concatenate(own_at + halo_at, axis=1)
    keys = seg.shape[1]
    tokens = SIDE * 128
    number = lax.broadcasted_iota(jnp.int32, (128, keys), 0).astype(F32)
    docs = spread_rows(seg_doc[...].astype(F32))
    docs = jnp.concatenate([docs] * (keys // 128), axis=1)
    doc = jnp.sum(jnp.where(number == seg, docs, 0.0), axis=0, keepdims=True)
    order = jnp.where(seg < 0.0, 65536.0 + at, doc * 2048.0 + at)
    tall, tall_seg = spread_rows(order), spread_rows(seg)
    key_rank, rank, pos = [], [], []
    for c in range(keys // 128):
        cut = slice(128 * c, 128 * (c + 1))
        less = tall < order[:, cut]
        key_rank.append(count(less))
        if c < SIDE:
            rank.append(count(less[:tokens]))
            pos.append(count(less & (tall_seg == seg[:, cut])))
    key_rank, rank, pos = [jnp.concatenate(v, axis=1) for v in (key_rank, rank, pos)]
    doc = doc[:, :tokens]
    low, high = jnp.zeros_like(doc), jnp.zeros_like(doc)
    for d in range(doc_lens.shape[0]):
        length = doc_lens[d].astype(F32)
        low = low + jnp.where(doc > d, length, 0.0)
        high = high + jnp.where(doc >= d, length, 0.0)
    mine = key_rank[:, :tokens]
    ranges = [low, high, mine - pos, mine + 1.0]
    coarse = [jnp.floor(v * (1.0 / 64.0)) for v in ranges]
    fine = [v - 64.0 * c for v, c in zip(ranges, coarse)]
    table = jnp.concatenate(coarse + fine + [rank] * 8, axis=0)
    return table, jnp.concatenate([key_rank] * 8, axis=0), pos


def gather_project(
    hid, gain, inverse, seg_ids, seg_doc, doc_lens, wq, wkv, pfx, wo,
    q_out, kv, pfx_all, wo_all, table, key_table,
    xs, wqs, wkvs, cos, sin, send, recv, x_send, x_recv, halo_send, halo_recv, stay,
):
    x, core, z, y = place()
    here = lambda dx, dcore, dz, dy: device(
        x + dx, core if dcore == 0 else 1 - core, z + dz, y + dy
    )
    down = SIDE - 1
    stays = [
        pltpu.make_async_copy(own, every.at[y], stay.at[k])
        for k, (own, every) in enumerate([(wkv, wkvs), (wq, wqs), (pfx, pfx_all), (wo, wo_all)])
    ]
    for copy in stays:
        copy.start()
    greet([
        here(0, 0, 0, 1), here(0, 0, 0, down), here(0, 0, 1, 0), here(0, 0, down, 0),
        here(1, 0, 0, 0), here(down, 0, 0, 0), here(0, 1, 0, 0),
    ])

    def pieces(own, every, step, size, offset=0, cols=None):
        across = slice(None) if cols is None else pl.ds(*cols)

        def at(n):
            return pl.ds(pl.multiple_of(n * step + offset, size), size)

        return lambda n: own.at[at(n), across], lambda s, n: every.at[s, at(n), across]

    parts = [
        pieces(wkv, wkvs, 512, 512),
        pieces(wq, wqs, 512, 256),
        pieces(wq, wqs, 512, 256, 256),
        pieces(pfx, pfx_all, 512, 512),
        pieces(wo, wo_all, 32, 32, 0, (0, 2048)),
        pieces(wo, wo_all, 32, 32, 0, (2048, 2048)),
    ]
    units = [Spread(own, every, send.at[k], recv.at[k]) for k, (own, every) in enumerate(parts)]
    units[0].start()

    values = hid[...].astype(F32)
    scale = lax.rsqrt(jnp.mean(values * values, axis=-1, keepdims=True) + EPS)
    xs[z] = (values * scale * gain[...].astype(F32)).astype(BF16)

    per_half = HALO // PIECE

    def x_copy(side, n, d=0):
        view = xs.at[(z + d) % SIDE, pl.ds(PIECE * n, PIECE), :]
        i = n + (2 * per_half if d else 0)
        to = here(0, 0, down if side else 1, 0)
        return remote(view, view, x_send.at[side, i], x_recv.at[side, i], to)

    def first_half(side, k):
        return (k + per_half * side) % (2 * per_half)

    def x_own(k):
        if k < 2 * per_half:
            for side in range(2):
                x_copy(side, first_half(side, k)).start()

    def x_got(k):
        for side in range(2):
            d = 1 if side else down
            if k < 2 * per_half:
                n = first_half(side, k)
                view = xs.at[(z + d) % SIDE, pl.ds(PIECE * n, PIECE), :]
                i = n
            else:
                n = first_half(side, k - 2 * per_half)
                view = xs.at[(z + 2) % SIDE, pl.ds(PIECE * n, PIECE), :]
                i = n + 2 * per_half
            remote(view, view, x_send.at[side, i], x_recv.at[side, i], here(0, 0, 1, 0)).wait_recv()
            if k < per_half:
                x_copy(side, n, d).start()

    tokens = SIDE * 128
    half_rows = 2 * 128

    def project_kv():
        for s in range(SIDE):
            @pl.loop(0, 2)
            def _(m):
                tall = pl.ds(pl.multiple_of(m * half_rows, half_rows), half_rows)
                lhs = xs[pl.ds(2 * m, 2)].reshape(half_rows, xs.shape[2])
                got = jnp.dot(lhs, wkvs[s], preferred_element_type=F32)
                if s % 2 == 0:
                    got = rotate(got, cos[tall, :], sin[tall, :])
                kv[tall, pl.ds(HEAD * s, HEAD)] = got.astype(BF16)

    def project_q(s):
        @pl.loop(0, 2)
        def _(m):
            tall = pl.ds(pl.multiple_of(m * half_rows, half_rows), half_rows)
            lhs = xs[pl.ds(2 * m, 2)].reshape(half_rows, xs.shape[2])
            got = jnp.dot(lhs, wqs[s], preferred_element_type=F32)
            for n in range(2):
                one = rotate(got[:, HEAD * n : HEAD * (n + 1)], cos[tall, :], sin[tall, :])
                q_out[tall, pl.ds(HEAD * (2 * s + n), HEAD)] = one.astype(BF16)

    def halo_copy(slot):
        dst = (slot + y // 3) % SIDE
        return remote(
            kv.at[pl.ds(128 * slot + HALO, HALO), :],
            kv.at[pl.ds(pl.multiple_of(tokens + HALO * dst, HALO), HALO), :],
            halo_send.at[slot],
            halo_recv.at[slot],
            here(0, 0, 0, 1),
        )

    def describe_tokens():
        rows, key_rows, pos = describe(seg_ids, seg_doc, doc_lens, y)
        table[...] = rows
        key_table[...] = key_rows
        angle = (pfx.shape[0] + spread_rows(pos)) * inverse[...]
        cos[...] = jnp.cos(angle)
        lane = lax.broadcasted_iota(jnp.int32, angle.shape, 1)
        turn = jnp.sin(angle)
        sin[...] = jnp.where(lane < HEAD // 2, -turn, turn)

    def keys_and_values():
        for k in range(2):
            stays[k].wait()
        for unit in units[:3]:
            unit.sibling()
        project_kv()
        for slot in range(SIDE):
            halo_copy(slot).start()

    extra = {3: describe_tokens, 12: keys_and_values}
    for s in range(SIDE):
        extra[13 + s] = functools.partial(project_q, s)
    lag = 2
    ahead = 3
    for k in range(ahead):
        x_own(k)
    for t in range(3 * len(units) + lag):
        if t < 3 * len(units):
            for i in Y_ROUNDS[t % 3]:
                units[t // 3].along_y(i)
            if t % 3 == 0 and t // 3 + 1 < len(units):
                units[t // 3 + 1].start()
        if t < 3 * per_half:
            x_got(t)
            x_own(t + ahead)
        if t >= lag:
            for i in X_ROUNDS[(t - lag) % 3]:
                units[(t - lag) // 3].along_x(i)
        if t in extra:
            extra[t]()
    for unit in units[3:]:
        unit.sibling()
    for k in range(2, 4):
        stays[k].wait()
    for slot in range(SIDE):
        halo_copy(slot).wait()
    for side in range(2):
        for n in range(2 * per_half):
            x_copy(side, n).wait_send()
        for k in range(per_half):
            x_copy(side, first_half(side, k), 1 if side else down).wait_send()
    for unit in units:
        unit.sent()


def attend(table, key_table, q, kv, pfx, out, perm, qs, kvs, ranges, outs, top, total, acc):
    tokens, news, prefix = q.shape[0], kv.shape[0], pfx.shape[1]
    tile, keys, group = 64, 256, 4
    lanes = group * tile
    exponent = math.log2(math.e) / math.sqrt(HEAD)

    def one_hot(flags):
        return jnp.where(flags, 1.0, 0.0).astype(BF16)

    rank = table[8:9, :]
    spots = lax.broadcasted_iota(jnp.int32, (tokens, tokens), 0).astype(F32)
    qs[...] = jnp.dot(one_hot(spots == rank), q[...], preferred_element_type=F32).astype(BF16)
    spots = lax.broadcasted_iota(jnp.int32, (news, news), 0).astype(F32)
    kvs[...] = jnp.dot(
        one_hot(spots == key_table[0:1, :]), kv[...], preferred_element_type=F32
    ).astype(BF16)
    tall = spread_rows(rank)
    lane = lax.broadcasted_iota(jnp.int32, (tokens, 128), 1)
    rows = table[...].astype(BF16)
    for i in range(tokens // tile):
        flags = one_hot(tall == ((lane % tile) + tile * i).astype(F32))
        got = jnp.dot(rows, flags, preferred_element_type=F32)
        got = 64.0 * got[0:8] + jnp.concatenate([got[4:8]] * 2, axis=0)
        ranges[i] = jnp.concatenate([got] * (lanes // 128), axis=1)
    for c in range(tokens // 128):
        perm[:, pl.ds(128 * c, 128)] = one_hot(tall == (lane + 128 * c).astype(F32))

    @pl.loop(0, tokens // tile)
    def _(i):
        cut = pl.ds(pl.multiple_of(i * tile, tile), tile)
        top[...] = jnp.full(top.shape, MASKED, F32)
        total[...] = jnp.zeros(total.shape, F32)
        acc[...] = jnp.zeros(acc.shape, F32)
        queries = [
            jnp.concatenate(
                [qs[cut, pl.ds(HEAD * (group * h + n), HEAD)] for n in range(group)], axis=0
            )
            for h in range(2)
        ]

        def sweep(low, high, size, load):
            first = jnp.min(low).astype(jnp.int32) // 128 * 128
            last = jnp.max(high).astype(jnp.int32)

            @pl.loop(0, (last - first + keys - 1) // keys)
            def _(j):
                begin = first + j * keys
                start = pl.multiple_of(jnp.minimum(begin, size - keys), 128)
                at = lax.broadcasted_iota(jnp.int32, (keys, lanes), 0)
                near = jnp.maximum(low.astype(jnp.int32), begin) - start
                far = high.astype(jnp.int32) - start
                allowed = (at >= near) & (at < far)
                for h in range(2):
                    key, value = load(h, pl.ds(start, keys))
                    s = lax.dot_general(
                        key, queries[h], (((1,), (1,)), ((), ())), preferred_element_type=F32
                    )
                    s = jnp.where(allowed, s * exponent, MASKED)
                    old = top[h, 0:1, :]
                    new = jnp.maximum(old, jnp.max(s, axis=0, keepdims=True))
                    p = jnp.exp2(s - new)
                    fade = jnp.exp2(old - new)
                    top[h, 0:1, :] = new
                    total[h, 0:1, :] = total[h, 0:1, :] * fade + jnp.sum(p, axis=0, keepdims=True)
                    acc[h] = acc[h] * fade + lax.dot_general(
                        value, p.astype(BF16), (((0,), (0,)), ((), ())), preferred_element_type=F32
                    )

        got = ranges[i]
        sweep(
            got[2:3],
            got[3:4],
            news,
            lambda h, at: (
                kvs[at, pl.ds(2 * HEAD * h, HEAD)],
                kvs[at, pl.ds(2 * HEAD * h + HEAD, HEAD)],
            ),
        )
        sweep(got[0:1], got[1:2], prefix, lambda h, at: (pfx[2 * h, at, :], pfx[2 * h + 1, at, :]))
        for h in range(2):
            done = jnp.transpose(acc[h] / total[h, 0:1, :]).astype(BF16)
            for n in range(group):
                outs[cut, pl.ds(HEAD * (group * h + n), HEAD)] = done[n * tile : (n + 1) * tile]

    out[...] = jnp.dot(perm[...], outs[...], preferred_element_type=F32).astype(BF16)


COLS = 512


def project_reduce(
    att, wo, hid, mixed,
    far_out, near_out, far_in, near_in, far_send, far_recv, near_send, near_recv,
):
    x, core, z, y = place()
    sides = [device(x, core, z + 1, y), device(x, core, z + SIDE - 1, y)]
    greet(sides)
    chunks = wo.shape[1] // COLS

    def partial(slot, j):
        return jnp.dot(
            att[slot % SIDE], wo[:, pl.ds(COLS * j, COLS)], preferred_element_type=F32
        )

    def far(j):
        return remote(
            far_out.at[j], far_in.at[j], far_send.at[j], far_recv.at[j], sides[j % 2]
        )

    def near(side, j):
        return remote(
            near_out.at[side, j],
            near_in.at[side, j],
            near_send.at[side, j],
            near_recv.at[side, j],
            sides[side],
        )

    for j in range(chunks):
        far_out[j] = partial(z + 2, j).astype(BF16)
        far(j).start()
    for j in range(chunks):
        side = 1 - j % 2
        near_out[side, j] = partial(z + (3 if side else 1), j).astype(BF16)
        near(side, j).start()
        side = j % 2
        mine = partial(z + (3 if side else 1), j)
        far(j).wait_recv()
        near_out[side, j] = (mine + far_in[j].astype(F32)).astype(BF16)
        near(side, j).start()
    for j in range(chunks):
        cut = pl.ds(COLS * j, COLS)
        mine = partial(z, j) + hid[:, cut].astype(F32)
        near(0, j).wait_recv()
        near(1, j).wait_recv()
        mine = mine + near_in[0, j].astype(F32) + near_in[1, j].astype(F32)
        mixed[:, cut] = mine.astype(BF16)
    for j in range(chunks):
        far(j).wait_send()
        near(0, j).wait_send()
        near(1, j).wait_send()


def local(hidden_in, norm_gain, w_query, keyvalue_weight, w_out, cache, seg_ids, seg_doc, doc_lens):
    prefix_len = cache.shape[0]
    width = hidden_in.shape[1]
    inverse = THETA ** (-(np.arange(HEAD // 2, dtype=np.float64) * 2.0 / HEAD))
    inverse = jnp.asarray(np.concatenate([inverse, inverse])[None, :], F32)

    vmem = pl.BlockSpec(memory_space=pltpu.VMEM)
    smem = pl.BlockSpec(memory_space=pltpu.SMEM)
    whole = pl.BlockSpec(memory_space=pl.ANY)
    tokens = SIDE * 128
    news = tokens + SIDE * HALO
    q, kv, pfx, wo, table, key_table = pl.pallas_call(
        gather_project,
        out_shape=(
            jax.ShapeDtypeStruct((tokens, 8 * HEAD), BF16),
            jax.ShapeDtypeStruct((news, 4 * HEAD), BF16),
            jax.ShapeDtypeStruct((SIDE, prefix_len, HEAD), BF16),
            jax.ShapeDtypeStruct((SIDE,) + w_out.shape, BF16),
            jax.ShapeDtypeStruct((16, tokens), F32),
            jax.ShapeDtypeStruct((8, news), F32),
        ),
        in_specs=[vmem] * 5 + [smem] + [whole] * 4,
        out_specs=(vmem,) * 6,
        scratch_shapes=[
            pltpu.VMEM((SIDE, 128, width), BF16),
            pltpu.VMEM((SIDE,) + w_query.shape, BF16),
            pltpu.VMEM((SIDE,) + keyvalue_weight.shape, BF16),
            pltpu.VMEM((tokens, HEAD), F32),
            pltpu.VMEM((tokens, HEAD), F32),
            pltpu.SemaphoreType.DMA((6, 24)),
            pltpu.SemaphoreType.DMA((6, 24)),
            pltpu.SemaphoreType.DMA((2, 16)),
            pltpu.SemaphoreType.DMA((2, 16)),
            pltpu.SemaphoreType.DMA((4,)),
            pltpu.SemaphoreType.DMA((4,)),
            pltpu.SemaphoreType.DMA((4,)),
        ],
        compiler_params=pltpu.CompilerParams(
            collective_id=0, has_side_effects=True, vmem_limit_bytes=36 * 2**20
        ),
        name="gather_project",
    )(
        hidden_in,
        norm_gain[None, :],
        inverse,
        seg_ids[None, :],
        seg_doc[None, :],
        doc_lens,
        w_query,
        keyvalue_weight,
        cache,
        w_out,
    )

    attended = pl.pallas_call(
        attend,
        out_shape=jax.ShapeDtypeStruct((tokens, 8 * HEAD), BF16),
        in_specs=[vmem] * 5,
        out_specs=vmem,
        scratch_shapes=[
            pltpu.VMEM((tokens, tokens), BF16),
            pltpu.VMEM((tokens, 8 * HEAD), BF16),
            pltpu.VMEM((news, 4 * HEAD), BF16),
            pltpu.VMEM((8, 8, 256), F32),
            pltpu.VMEM((tokens, 8 * HEAD), BF16),
            pltpu.VMEM((2, 8, 256), F32),
            pltpu.VMEM((2, 8, 256), F32),
            pltpu.VMEM((2, HEAD, 256), F32),
        ],
        compiler_params=pltpu.CompilerParams(vmem_limit_bytes=32 * 2**20),
        name="attend",
    )(table, key_table, q, kv, pfx)

    chunks = width // COLS
    return pl.pallas_call(
        project_reduce,
        out_shape=jax.ShapeDtypeStruct(hidden_in.shape, BF16),
        in_specs=[vmem] * 3,
        out_specs=vmem,
        scratch_shapes=[
            pltpu.VMEM((chunks, 128, COLS), BF16),
            pltpu.VMEM((2, chunks, 128, COLS), BF16),
            pltpu.VMEM((chunks, 128, COLS), BF16),
            pltpu.VMEM((2, chunks, 128, COLS), BF16),
            pltpu.SemaphoreType.DMA((chunks,)),
            pltpu.SemaphoreType.DMA((chunks,)),
            pltpu.SemaphoreType.DMA((2, chunks)),
            pltpu.SemaphoreType.DMA((2, chunks)),
        ],
        compiler_params=pltpu.CompilerParams(
            collective_id=1, has_side_effects=True, vmem_limit_bytes=32 * 2**20
        ),
        name="project_reduce",
    )(attended.reshape(SIDE, 128, 8 * HEAD), wo.reshape(-1, width), hidden_in)


def solution(mesh):
    return jax.shard_map(
        local,
        mesh=mesh,
        in_specs=(
            P(("dp", "tensor"), None),
            P(),
            P(None, "tensor"),
            P(None, "tensor"),
            P("tensor", None),
            P(None, "tensor"),
            P("dp"),
            P("dp"),
            P(),
        ),
        out_specs=P(("dp", "tensor"), None),
        check_vma=False,
    )
```

```python
import functools
import math

import jax
import jax.numpy as jnp
from jax import lax
from jax.experimental import pallas as pl
from jax.experimental.pallas import tpu as pltpu
from jax.sharding import PartitionSpec as P

HEAD = 128
HALO = 64
SIDE = 4
EPS = 1e-05
THETA = 500000.0
MASKED = -1e30
MESH = pl.DeviceIdType.MESH
BF16 = jnp.bfloat16
F32 = jnp.float32


def place():
    dp, tensor = lax.axis_index("dp"), lax.axis_index("tensor")
    return dp // 2, dp % 2, tensor // SIDE, tensor % SIDE


def device(x, core, z, y):
    return (2 * (x % SIDE) + core, SIDE * (z % SIDE) + y % SIDE)


def greet(others):
    barrier = pltpu.get_barrier_semaphore()
    for other in others:
        pl.semaphore_signal(barrier, inc=1, device_id=other, device_id_type=MESH)
    pl.semaphore_wait(barrier, len(others))


def remote(src, dst, send, recv, other):
    return pltpu.make_async_remote_copy(
        src_ref=src, dst_ref=dst, send_sem=send, recv_sem=recv, device_id=other, device_id_type=MESH
    )


def rotate(v, cos, sin):
    return v * cos + pltpu.roll(v, HEAD // 2, 1) * sin


def pieces(own, every, step, size, offset=0, cols=None):
    across = slice(None) if cols is None else pl.ds(*cols)

    def at(n):
        return pl.ds(pl.multiple_of(n * step + offset, size), size)

    return lambda n: own.at[at(n), across], lambda s, n: every.at[s, at(n), :]


class Spread:
    def __init__(self, own, block, bulk, send, recv):
        self.own, self.block, self.bulk, self.send, self.recv = own, block, bulk, send, recv
        self.x, self.core, self.z, self.y = place()

    def number(self, parity, core, half):
        return 4 * parity + 2 * core + half

    def up(self, n):
        return (self.x, self.core, self.z, self.y + n)

    def copy(self, i, d, piece, to, first=False):
        slot = (self.y + d + SIDE) % SIDE
        src = self.own(piece) if first else self.block(slot, piece)
        return remote(
            src, self.block(slot, piece), self.send, self.recv.at[min(i, 12)], device(*to)
        )

    def mine(self, half):
        return self.number(self.x % 2, self.core, half)

    def sends(self, i):
        if i in (0, 1):
            return self.copy(i, 0, self.mine(i), self.up(1), True)
        if i == 2:
            return self.copy(i, 3, self.mine(0), self.up(1))
        if i in (3, 4):
            return self.copy(i, 0, self.mine(4 - i), self.up(SIDE - 1), True)
        if i == 5:
            return self.copy(i, 1, self.mine(1), self.up(SIDE - 1))
        d, half = 1 + (i % 6) // 2, i % 2
        if i < 12:
            to = (self.x + (SIDE - 1 if half else 1), self.core, self.z, self.y)
            return self.copy(i, d, self.mine(half), to)
        parity = self.x % 2 if i < 18 else 1 - self.x % 2
        piece = self.number(parity, self.core, half)
        return self.copy(i, d, piece, (self.x, 1 - self.core, self.z, self.y))

    def got(self, i):
        if i < 6:
            d = {0: 3, 1: 3, 2: 2, 3: 1, 4: 1, 5: 2}[i]
            half = {0: 0, 1: 1, 2: 0, 3: 1, 4: 0, 5: 1}[i]
            piece = self.mine(half)
        else:
            d, half = 1 + (i % 6) // 2, i % 2
            piece = self.number(1 - self.x % 2, self.core, half)
        view = self.block((self.y + d) % SIDE, piece)
        remote(view, view, self.send, self.recv.at[i], device(*self.up(1))).wait_recv()

    def start(self):
        for i in (0, 3, 1, 4):
            self.sends(i).start()

    def along_y(self, i):
        self.got(i)
        if i == 0:
            self.sends(2).start()
        if i == 3:
            self.sends(5).start()
        d = {0: 3, 1: 3, 2: 2, 3: 1, 4: 1, 5: 2}[i]
        half = {0: 0, 1: 1, 2: 0, 3: 1, 4: 0, 5: 1}[i]
        self.sends(6 + 2 * (d - 1) + half).start()
        self.sends(12 + 2 * (d - 1) + half).start()

    def along_x(self, i):
        self.got(i)
        self.sends(i + 12).start()

    def sibling(self):
        view = self.bulk(1)
        remote(view, view, self.send, self.recv.at[12], device(*self.up(1))).wait_recv()

    def sent(self):
        view = self.bulk(2)
        remote(view, view, self.send, self.recv.at[12], device(*self.up(1))).wait_send()


Y_ROUNDS = ((0, 3), (1, 4), (2, 5))
X_ROUNDS = ((10, 7), (11, 6), (8, 9))
PIECE = 16


def spread_rows(row):
    return jnp.transpose(jnp.broadcast_to(row, (128, row.shape[1])))


def count(flags):
    return jnp.sum(jnp.where(flags, 1.0, 0.0), axis=0, keepdims=True)


def describe(seg_ids, seg_doc, doc_lens, y):
    lane = lax.broadcasted_iota(jnp.int32, (1, 128), 1)

    def window(n):
        return seg_ids[:, pl.ds(pl.multiple_of(128 * jnp.maximum(n, 0), 128), 128)].astype(F32)

    own = [window(SIDE * s + y) for s in range(SIDE)]
    own_at = [(128 * (SIDE * s + y) + lane).astype(F32) for s in range(SIDE)]
    halo, halo_at = [], []
    for s in (0, 2):
        low, high = window(SIDE * s + y - 1), window(SIDE * (s + 1) + y - 1)
        both = jnp.where(lane < HALO, pltpu.roll(low, HALO, 1), high)
        start = jnp.where(
            lane < HALO, 128 * (SIDE * s + y) - HALO, 128 * (SIDE * (s + 1) + y) - 2 * HALO
        )
        at = (start + lane).astype(F32)
        halo.append(jnp.where(at < 0.0, -1.0, both))
        halo_at.append(at)
    seg = jnp.concatenate(own + halo, axis=1)
    at = jnp.concatenate(own_at + halo_at, axis=1)
    keys = seg.shape[1]
    tokens = SIDE * 128
    number = lax.broadcasted_iota(jnp.int32, (128, keys), 0).astype(F32)
    docs = spread_rows(seg_doc[...].astype(F32))
    docs = jnp.concatenate([docs] * (keys // 128), axis=1)
    doc = jnp.sum(jnp.where(number == seg, docs, 0.0), axis=0, keepdims=True)
    order = jnp.where(seg < 0.0, 65536.0 + at, doc * 2048.0 + at)
    tall, tall_seg = spread_rows(order), spread_rows(seg)
    key_rank, rank, pos = [], [], []
    for c in range(keys // 128):
        cut = slice(128 * c, 128 * (c + 1))
        less = tall < order[:, cut]
        key_rank.append(count(less))
        if c < SIDE:
            rank.append(count(less[:tokens]))
            pos.append(count(less & (tall_seg == seg[:, cut])))
    key_rank, rank, pos = [jnp.concatenate(v, axis=1) for v in (key_rank, rank, pos)]
    doc = doc[:, :tokens]
    low, high = jnp.zeros_like(doc), jnp.zeros_like(doc)
    for d in range(doc_lens.shape[0]):
        length = doc_lens[d].astype(F32)
        low = low + jnp.where(doc > d, length, 0.0)
        high = high + jnp.where(doc >= d, length, 0.0)
    mine = key_rank[:, :tokens]
    ranges = [low, high, mine - pos, mine + 1.0]
    coarse = [jnp.floor(v * (1.0 / 64.0)) for v in ranges]
    fine = [v - 64.0 * c for v, c in zip(ranges, coarse)]
    table = jnp.concatenate(coarse + fine + [rank] * 8, axis=0)
    return table, jnp.concatenate([key_rank] * 8, axis=0), pos


def gather_project(
    gain, hid_far, seg_ids_far, seg_doc_far, doc_lens_far, wq, wkv, pfx, wo,
    q_out, kv, pfx_all, wo_low, table, key_table,
    xs, wqs, wkvs, cos, sin, hid, seg_ids, seg_doc, doc_lens,
    send, recv, x_send, x_recv, halo_send, halo_recv, stay,
):
    x, core, z, y = place()
    here = lambda dx, dcore, dz, dy: device(
        x + dx, core if dcore == 0 else 1 - core, z + dz, y + dy
    )
    down = SIDE - 1
    stays = [
        pltpu.make_async_copy(src, dst, stay.at[k])
        for k, (src, dst) in enumerate(
            [
                (hid_far, hid),
                (seg_ids_far, seg_ids),
                (seg_doc_far, seg_doc),
                (doc_lens_far, doc_lens),
                (wkv, wkvs.at[y]),
                (wq, wqs.at[y]),
                (pfx, pfx_all.at[y]),
                (wo.at[:, pl.ds(0, wo_low.shape[2])], wo_low.at[y]),
            ]
        )
    ]
    for copy in stays:
        copy.start()
    greet([
        here(0, 0, 0, 1), here(0, 0, 0, down), here(0, 0, 1, 0), here(0, 0, down, 0),
        here(1, 0, 0, 0), here(down, 0, 0, 0), here(0, 1, 0, 0),
    ])

    def third(array, size):
        return lambda n: array.at[pl.ds(0, 3), pl.ds(0, n * size), :]

    parts = [
        pieces(wkv, wkvs, 512, 512) + (third(wkvs, 2048),),
        pieces(wq, wqs, 512, 256) + (third(wqs, 1024),),
        pieces(wq, wqs, 512, 256, 256) + (third(wqs, 1024),),
        pieces(pfx, pfx_all, 512, 512) + (third(pfx_all, 2048),),
        pieces(wo, wo_low, 32, 32, 0, (0, wo_low.shape[2])) + (third(wo_low, 128),),
    ]
    units = [Spread(*part, send.at[k], recv.at[k]) for k, part in enumerate(parts)]
    units[0].start()

    stays[0].wait()
    values = hid[...].astype(F32)
    scale = lax.rsqrt(jnp.mean(values * values, axis=-1, keepdims=True) + EPS)
    xs[z] = (values * scale * gain[...].astype(F32)).astype(BF16)

    per_half = HALO // PIECE

    def x_copy(side, n, d=0):
        view = xs.at[(z + d) % SIDE, pl.ds(PIECE * n, PIECE), :]
        i = n + (2 * per_half if d else 0)
        to = here(0, 0, down if side else 1, 0)
        return remote(view, view, x_send.at[side], x_recv.at[side, i], to)

    def first_half(side, k):
        return (k + per_half * side) % (2 * per_half)

    def x_own(k):
        if k < 2 * per_half:
            for side in range(2):
                x_copy(side, first_half(side, k)).start()

    def x_got(k):
        for side in range(2):
            d = 1 if side else down
            if k < 2 * per_half:
                n = first_half(side, k)
                view = xs.at[(z + d) % SIDE, pl.ds(PIECE * n, PIECE), :]
                i = n
            else:
                n = first_half(side, k - 2 * per_half)
                view = xs.at[(z + 2) % SIDE, pl.ds(PIECE * n, PIECE), :]
                i = n + 2 * per_half
            remote(view, view, x_send.at[side], x_recv.at[side, i], here(0, 0, 1, 0)).wait_recv()
            if k < per_half:
                x_copy(side, n, d).start()

    tokens = SIDE * 128
    half_rows = 2 * 128

    def project_kv():
        for s in range(SIDE):
            @pl.loop(0, 2)
            def _(m):
                tall = pl.ds(pl.multiple_of(m * half_rows, half_rows), half_rows)
                lhs = xs[pl.ds(2 * m, 2)].reshape(half_rows, xs.shape[2])
                got = jnp.dot(lhs, wkvs[s], preferred_element_type=F32)
                if s % 2 == 0:
                    got = rotate(got, cos[tall, :], sin[tall, :])
                kv[tall, pl.ds(HEAD * s, HEAD)] = got.astype(BF16)

    def project_q(s):
        @pl.loop(0, 2)
        def _(m):
            tall = pl.ds(pl.multiple_of(m * half_rows, half_rows), half_rows)
            lhs = xs[pl.ds(2 * m, 2)].reshape(half_rows, xs.shape[2])
            got = jnp.dot(lhs, wqs[s], preferred_element_type=F32)
            for n in range(2):
                one = rotate(got[:, HEAD * n : HEAD * (n + 1)], cos[tall, :], sin[tall, :])
                q_out[tall, pl.ds(HEAD * (2 * s + n), HEAD)] = one.astype(BF16)

    def halo_copy(slot):
        dst = (slot + y // 3) % SIDE
        return remote(
            kv.at[pl.ds(128 * slot + HALO, HALO), :],
            kv.at[pl.ds(pl.multiple_of(tokens + HALO * dst, HALO), HALO), :],
            halo_send.at[slot],
            halo_recv.at[slot],
            here(0, 0, 0, 1),
        )

    def describe_tokens():
        for k in range(1, 4):
            stays[k].wait()
        rows, key_rows, pos = describe(seg_ids, seg_doc, doc_lens, y)
        table[...] = rows
        key_table[...] = key_rows
        lane = lax.broadcasted_iota(jnp.int32, (1, HEAD), 1)
        inverse = jnp.zeros((1, HEAD), F32)
        for i in range(HEAD // 2):
            inverse = jnp.where(lane % (HEAD // 2) == i, THETA ** (-2.0 * i / HEAD), inverse)
        angle = (pfx.shape[0] + spread_rows(pos)) * inverse
        cos[...] = jnp.cos(angle)
        turn = jnp.sin(angle)
        sin[...] = jnp.where(lane < HEAD // 2, -turn, turn)

    def keys_and_values():
        for k in range(4, 6):
            stays[k].wait()
        for unit in units[:3]:
            unit.sibling()
        project_kv()
        for slot in range(SIDE):
            halo_copy(slot).start()

    extra = {3: describe_tokens, 12: keys_and_values}
    for s in range(SIDE):
        extra[13 + s] = functools.partial(project_q, s)
    lag = 2
    ahead = 3
    for k in range(ahead):
        x_own(k)
    for t in range(3 * len(units) + lag):
        if t < 3 * len(units):
            for i in Y_ROUNDS[t % 3]:
                units[t // 3].along_y(i)
            if t % 3 == 0 and t // 3 + 1 < len(units):
                units[t // 3 + 1].start()
        if t < 3 * per_half:
            x_got(t)
            x_own(t + ahead)
        if t >= lag:
            for i in X_ROUNDS[(t - lag) % 3]:
                units[(t - lag) // 3].along_x(i)
        if t in extra:
            extra[t]()
    for unit in units[3:]:
        unit.sibling()
    for k in range(6, 8):
        stays[k].wait()
    for slot in range(SIDE):
        halo_copy(slot).wait()
    for side in range(2):
        view = xs.at[pl.ds(0, 3), pl.ds(0, HALO), :]
        remote(view, view, x_send.at[side], x_recv.at[side, 0], here(0, 0, 1, 0)).wait_send()
    for unit in units:
        unit.sent()


def attend(table, key_table, q, kv, pfx, out, perm, qs, kvs, ranges, outs, top, total, acc):
    tokens, news, prefix = q.shape[0], kv.shape[0], pfx.shape[1]
    tile, keys, group = 64, 256, 4
    lanes = group * tile
    exponent = math.log2(math.e) / math.sqrt(HEAD)

    def one_hot(flags):
        return jnp.where(flags, 1.0, 0.0).astype(BF16)

    rank = table[8:9, :]
    spots = lax.broadcasted_iota(jnp.int32, (tokens, tokens), 0).astype(F32)
    qs[...] = jnp.dot(one_hot(spots == rank), q[...], preferred_element_type=F32).astype(BF16)
    spots = lax.broadcasted_iota(jnp.int32, (news, news), 0).astype(F32)
    kvs[...] = jnp.dot(
        one_hot(spots == key_table[0:1, :]), kv[...], preferred_element_type=F32
    ).astype(BF16)
    tall = spread_rows(rank)
    lane = lax.broadcasted_iota(jnp.int32, (tokens, 128), 1)
    rows = table[...].astype(BF16)
    for i in range(tokens // tile):
        flags = one_hot(tall == ((lane % tile) + tile * i).astype(F32))
        got = jnp.dot(rows, flags, preferred_element_type=F32)
        got = 64.0 * got[0:8] + jnp.concatenate([got[4:8]] * 2, axis=0)
        ranges[i] = jnp.concatenate([got] * (lanes // 128), axis=1)
    for c in range(tokens // 128):
        perm[:, pl.ds(128 * c, 128)] = one_hot(tall == (lane + 128 * c).astype(F32))

    @pl.loop(0, tokens // tile)
    def _(i):
        cut = pl.ds(pl.multiple_of(i * tile, tile), tile)
        top[...] = jnp.full(top.shape, MASKED, F32)
        total[...] = jnp.zeros(total.shape, F32)
        acc[...] = jnp.zeros(acc.shape, F32)
        queries = [
            jnp.concatenate(
                [qs[cut, pl.ds(HEAD * (group * h + n), HEAD)] for n in range(group)], axis=0
            )
            for h in range(2)
        ]

        def sweep(low, high, size, load):
            first = jnp.min(low).astype(jnp.int32) // 128 * 128
            last = jnp.max(high).astype(jnp.int32)

            @pl.loop(0, (last - first + keys - 1) // keys)
            def _(j):
                begin = first + j * keys
                start = pl.multiple_of(jnp.minimum(begin, size - keys), 128)
                at = lax.broadcasted_iota(jnp.int32, (keys, lanes), 0)
                near = jnp.maximum(low.astype(jnp.int32), begin) - start
                far = high.astype(jnp.int32) - start
                allowed = (at >= near) & (at < far)
                for h in range(2):
                    key, value = load(h, pl.ds(start, keys))
                    s = lax.dot_general(
                        key, queries[h], (((1,), (1,)), ((), ())), preferred_element_type=F32
                    )
                    s = jnp.where(allowed, s * exponent, MASKED)
                    old = top[h, 0:1, :]
                    new = jnp.maximum(old, jnp.max(s, axis=0, keepdims=True))
                    p = jnp.exp2(s - new)
                    fade = jnp.exp2(old - new)
                    top[h, 0:1, :] = new
                    total[h, 0:1, :] = total[h, 0:1, :] * fade + jnp.sum(p, axis=0, keepdims=True)
                    acc[h] = acc[h] * fade + lax.dot_general(
                        value, p.astype(BF16), (((0,), (0,)), ((), ())), preferred_element_type=F32
                    )

        got = ranges[i]
        sweep(
            got[2:3],
            got[3:4],
            news,
            lambda h, at: (
                kvs[at, pl.ds(2 * HEAD * h, HEAD)],
                kvs[at, pl.ds(2 * HEAD * h + HEAD, HEAD)],
            ),
        )
        sweep(got[0:1], got[1:2], prefix, lambda h, at: (pfx[2 * h, at, :], pfx[2 * h + 1, at, :]))
        for h in range(2):
            done = jnp.transpose(acc[h] / total[h, 0:1, :]).astype(BF16)
            for n in range(group):
                outs[cut, pl.ds(HEAD * (group * h + n), HEAD)] = done[n * tile : (n + 1) * tile]

    out[...] = jnp.dot(perm[...], outs[...], preferred_element_type=F32).astype(BF16)


COLS = 512


def project_reduce(
    att, wo_low, wo, hid_far, mixed,
    wo_high, hid, far_out, near_out, far_in, near_in,
    far_send, far_recv, near_send, near_recv, send, recv, stay,
):
    x, core, z, y = place()
    down = SIDE - 1
    sides = [device(x, core, z + 1, y), device(x, core, z + down, y)]
    half = wo_low.shape[2]
    stays = [
        pltpu.make_async_copy(wo.at[:, pl.ds(half, half)], wo_high.at[y], stay.at[0]),
        pltpu.make_async_copy(hid_far, hid, stay.at[1]),
    ]
    for copy in stays:
        copy.start()
    greet(
        sides
        + [device(x, core, z, y + 1), device(x, core, z, y + down)]
        + [device(x + 1, core, z, y), device(x + down, core, z, y), device(x, 1 - core, z, y)]
    )
    bulk = lambda n: wo_high.at[pl.ds(0, 3), pl.ds(0, 128 * n), :]
    unit = Spread(*pieces(wo, wo_high, 32, 32, 0, (half, half)), bulk, send.at[0], recv.at[0])
    unit.start()
    chunks = 2 * half // COLS

    def partial(slot, j):
        source, at = (wo_low, j) if j < chunks // 2 else (wo_high, j - chunks // 2)
        weight = source[:, :, pl.ds(COLS * at, COLS)].reshape(-1, COLS)
        return jnp.dot(att[slot % SIDE], weight, preferred_element_type=F32)

    def far(j):
        return remote(far_out.at[j], far_in.at[j], far_send.at[j], far_recv.at[j], sides[j % 2])

    def near(side, j):
        return remote(
            near_out.at[side, j],
            near_in.at[side, j],
            near_send.at[side, j],
            near_recv.at[side, j],
            sides[side],
        )

    def far_step(j):
        far_out[j] = partial(z + 2, j).astype(BF16)
        far(j).start()

    def near_step(j):
        side = 1 - j % 2
        near_out[side, j] = partial(z + (down if side else 1), j).astype(BF16)
        near(side, j).start()
        side = j % 2
        mine = partial(z + (down if side else 1), j)
        far(j).wait_recv()
        near_out[side, j] = (mine + far_in[j].astype(F32)).astype(BF16)
        near(side, j).start()

    def along_y(r):
        for i in Y_ROUNDS[r]:
            unit.along_y(i)

    def along_x(r):
        for i in X_ROUNDS[r]:
            unit.along_x(i)

    for j in range(chunks // 2):
        far_step(j)
    along_y(0)
    near_step(0)
    near_step(1)
    along_y(1)
    along_x(0)
    near_step(2)
    along_y(2)
    along_x(1)
    near_step(3)
    along_x(2)
    stays[0].wait()
    unit.sibling()
    for j in range(chunks // 2, chunks):
        far_step(j)
    for j in range(chunks // 2, chunks):
        near_step(j)
    stays[1].wait()
    for j in range(chunks):
        cut = pl.ds(COLS * j, COLS)
        mine = partial(z, j) + hid[:, cut].astype(F32)
        near(0, j).wait_recv()
        near(1, j).wait_recv()
        mine = mine + near_in[0, j].astype(F32) + near_in[1, j].astype(F32)
        mixed[:, cut] = mine.astype(BF16)
    for j in range(chunks):
        far(j).wait_send()
        near(0, j).wait_send()
        near(1, j).wait_send()
    unit.sent()


def local(hidden_in, norm_gain, w_query, keyvalue_weight, w_out, cache, seg_ids, seg_doc, doc_lens):
    prefix_len = cache.shape[0]
    width = hidden_in.shape[1]
    half = width // 2
    far = lambda array: pltpu.with_memory_space_constraint(array, pltpu.HBM)
    vmem = pl.BlockSpec(memory_space=pltpu.VMEM)
    whole = pl.BlockSpec(memory_space=pltpu.HBM)
    tokens = SIDE * 128
    news = tokens + SIDE * HALO
    q, kv, pfx, wo_low, table, key_table = pl.pallas_call(
        gather_project,
        out_shape=(
            jax.ShapeDtypeStruct((tokens, 8 * HEAD), BF16),
            jax.ShapeDtypeStruct((news, 4 * HEAD), BF16),
            jax.ShapeDtypeStruct((SIDE, prefix_len, HEAD), BF16),
            jax.ShapeDtypeStruct((SIDE, w_out.shape[0], half), BF16),
            jax.ShapeDtypeStruct((16, tokens), F32),
            jax.ShapeDtypeStruct((8, news), F32),
        ),
        in_specs=[vmem] + [whole] * 8,
        out_specs=(vmem,) * 6,
        scratch_shapes=[
            pltpu.VMEM((SIDE, 128, width), BF16),
            pltpu.VMEM((SIDE,) + w_query.shape, BF16),
            pltpu.VMEM((SIDE,) + keyvalue_weight.shape, BF16),
            pltpu.VMEM((tokens, HEAD), F32),
            pltpu.VMEM((tokens, HEAD), F32),
            pltpu.VMEM(hidden_in.shape, BF16),
            pltpu.VMEM((1,) + seg_ids.shape, jnp.int32),
            pltpu.VMEM((1,) + seg_doc.shape, jnp.int32),
            pltpu.SMEM(doc_lens.shape, jnp.int32),
            pltpu.SemaphoreType.DMA((5,)),
            pltpu.SemaphoreType.DMA((5, 13)),
            pltpu.SemaphoreType.DMA((2,)),
            pltpu.SemaphoreType.DMA((2, 16)),
            pltpu.SemaphoreType.DMA((4,)),
            pltpu.SemaphoreType.DMA((4,)),
            pltpu.SemaphoreType.DMA((8,)),
        ],
        compiler_params=pltpu.CompilerParams(
            collective_id=0, has_side_effects=True, vmem_limit_bytes=30 * 2**20
        ),
        name="gather_project",
    )(
        norm_gain[None, :],
        far(hidden_in),
        far(seg_ids[None, :]),
        far(seg_doc[None, :]),
        far(doc_lens),
        far(w_query),
        far(keyvalue_weight),
        far(cache),
        far(w_out),
    )

    attended = pl.pallas_call(
        attend,
        out_shape=jax.ShapeDtypeStruct((tokens, 8 * HEAD), BF16),
        in_specs=[vmem] * 5,
        out_specs=vmem,
        scratch_shapes=[
            pltpu.VMEM((tokens, tokens), BF16),
            pltpu.VMEM((tokens, 8 * HEAD), BF16),
            pltpu.VMEM((news, 4 * HEAD), BF16),
            pltpu.VMEM((8, 8, 256), F32),
            pltpu.VMEM((tokens, 8 * HEAD), BF16),
            pltpu.VMEM((2, 8, 256), F32),
            pltpu.VMEM((2, 8, 256), F32),
            pltpu.VMEM((2, HEAD, 256), F32),
        ],
        compiler_params=pltpu.CompilerParams(vmem_limit_bytes=32 * 2**20),
        name="attend",
    )(table, key_table, q, kv, pfx)

    chunks = width // COLS
    return pl.pallas_call(
        project_reduce,
        out_shape=jax.ShapeDtypeStruct(hidden_in.shape, BF16),
        in_specs=[vmem] * 2 + [whole] * 2,
        out_specs=vmem,
        scratch_shapes=[
            pltpu.VMEM((SIDE, w_out.shape[0], half), BF16),
            pltpu.VMEM(hidden_in.shape, BF16),
            pltpu.VMEM((chunks, 128, COLS), BF16),
            pltpu.VMEM((2, chunks, 128, COLS), BF16),
            pltpu.VMEM((chunks, 128, COLS), BF16),
            pltpu.VMEM((2, chunks, 128, COLS), BF16),
            pltpu.SemaphoreType.DMA((chunks,)),
            pltpu.SemaphoreType.DMA((chunks,)),
            pltpu.SemaphoreType.DMA((2, chunks)),
            pltpu.SemaphoreType.DMA((2, chunks)),
            pltpu.SemaphoreType.DMA((1,)),
            pltpu.SemaphoreType.DMA((1, 13)),
            pltpu.SemaphoreType.DMA((2,)),
        ],
        compiler_params=pltpu.CompilerParams(
            collective_id=1, has_side_effects=True, vmem_limit_bytes=32 * 2**20
        ),
        name="project_reduce",
    )(attended.reshape(SIDE, 128, 8 * HEAD), wo_low, far(w_out), far(hidden_in))


def solution(mesh):
    return jax.shard_map(
        local,
        mesh=mesh,
        in_specs=(
            P(("dp", "tensor"), None),
            P(),
            P(None, "tensor"),
            P(None, "tensor"),
            P("tensor", None),
            P(None, "tensor"),
            P("dp"),
            P("dp"),
            P(),
        ),
        out_specs=P(("dp", "tensor"), None),
        check_vma=False,
    )
```

```python
import functools
import math

import jax
import jax.numpy as jnp
from jax import lax
from jax.experimental import pallas as pl
from jax.experimental.pallas import tpu as pltpu
from jax.sharding import PartitionSpec as P

HEAD = 128
HALO = 64
SIDE = 4
EPS = 1e-05
THETA = 500000.0
MASKED = -1e30
MESH = pl.DeviceIdType.MESH
BF16 = jnp.bfloat16
F32 = jnp.float32


def place():
    dp, tensor = lax.axis_index("dp"), lax.axis_index("tensor")
    return dp // 2, dp % 2, tensor // SIDE, tensor % SIDE


def device(x, core, z, y):
    return (2 * (x % SIDE) + core, SIDE * (z % SIDE) + y % SIDE)


def greet(others):
    barrier = pltpu.get_barrier_semaphore()
    for other in others:
        pl.semaphore_signal(barrier, inc=1, device_id=other, device_id_type=MESH)
    pl.semaphore_wait(barrier, len(others))


def remote(src, dst, send, recv, other):
    return pltpu.make_async_remote_copy(
        src_ref=src, dst_ref=dst, send_sem=send, recv_sem=recv, device_id=other, device_id_type=MESH
    )


def rotate(v, cos, sin):
    return v * cos + pltpu.roll(v, HEAD // 2, 1) * sin


def pieces(own, every, step, size, offset=0, cols=None):
    across = slice(None) if cols is None else pl.ds(*cols)

    def at(n):
        return pl.ds(pl.multiple_of(n * step + offset, size), size)

    return lambda n: own.at[at(n), across], lambda s, n: every.at[s, at(n), :]


class Spread:
    def __init__(self, own, block, bulk, send, recv):
        self.own, self.block, self.bulk, self.send, self.recv = own, block, bulk, send, recv
        self.x, self.core, self.z, self.y = place()

    def number(self, parity, core, half):
        return 4 * parity + 2 * core + half

    def up(self, n):
        return (self.x, self.core, self.z, self.y + n)

    def copy(self, i, d, piece, to, first=False):
        slot = (self.y + d + SIDE) % SIDE
        src = self.own(piece) if first else self.block(slot, piece)
        return remote(
            src, self.block(slot, piece), self.send, self.recv.at[min(i, 12)], device(*to)
        )

    def mine(self, half):
        return self.number(self.x % 2, self.core, half)

    def sends(self, i):
        if i in (0, 1):
            return self.copy(i, 0, self.mine(i), self.up(1), True)
        if i == 2:
            return self.copy(i, 3, self.mine(0), self.up(1))
        if i in (3, 4):
            return self.copy(i, 0, self.mine(4 - i), self.up(SIDE - 1), True)
        if i == 5:
            return self.copy(i, 1, self.mine(1), self.up(SIDE - 1))
        d, half = 1 + (i % 6) // 2, i % 2
        if i < 12:
            to = (self.x + (SIDE - 1 if half else 1), self.core, self.z, self.y)
            return self.copy(i, d, self.mine(half), to)
        parity = self.x % 2 if i < 18 else 1 - self.x % 2
        piece = self.number(parity, self.core, half)
        return self.copy(i, d, piece, (self.x, 1 - self.core, self.z, self.y))

    def got(self, i):
        if i < 6:
            d = {0: 3, 1: 3, 2: 2, 3: 1, 4: 1, 5: 2}[i]
            half = {0: 0, 1: 1, 2: 0, 3: 1, 4: 0, 5: 1}[i]
            piece = self.mine(half)
        else:
            d, half = 1 + (i % 6) // 2, i % 2
            piece = self.number(1 - self.x % 2, self.core, half)
        view = self.block((self.y + d) % SIDE, piece)
        remote(view, view, self.send, self.recv.at[i], device(*self.up(1))).wait_recv()

    def start(self):
        for i in (0, 3, 1, 4):
            self.sends(i).start()

    def along_y(self, i):
        self.got(i)
        if i == 0:
            self.sends(2).start()
        if i == 3:
            self.sends(5).start()
        d = {0: 3, 1: 3, 2: 2, 3: 1, 4: 1, 5: 2}[i]
        half = {0: 0, 1: 1, 2: 0, 3: 1, 4: 0, 5: 1}[i]
        self.sends(6 + 2 * (d - 1) + half).start()
        self.sends(12 + 2 * (d - 1) + half).start()

    def along_x(self, i):
        self.got(i)
        self.sends(i + 12).start()

    def sibling(self):
        view = self.bulk(1)
        remote(view, view, self.send, self.recv.at[12], device(*self.up(1))).wait_recv()

    def sent(self):
        view = self.bulk(2)
        remote(view, view, self.send, self.recv.at[12], device(*self.up(1))).wait_send()


Y_ROUNDS = ((0, 3), (1, 4), (2, 5))
X_ROUNDS = ((10, 7), (11, 6), (8, 9))
PIECE = 16


def spread_rows(row):
    return jnp.transpose(jnp.broadcast_to(row, (128, row.shape[1])))


def count(flags):
    return jnp.sum(jnp.where(flags, 1.0, 0.0), axis=0, keepdims=True)


def describe(seg_ids, seg_doc, doc_lens, y):
    lane = lax.broadcasted_iota(jnp.int32, (1, 128), 1)

    def window(n):
        return seg_ids[:, pl.ds(pl.multiple_of(128 * jnp.maximum(n, 0), 128), 128)].astype(F32)

    own = [window(SIDE * s + y) for s in range(SIDE)]
    own_at = [(128 * (SIDE * s + y) + lane).astype(F32) for s in range(SIDE)]
    halo, halo_at = [], []
    for s in (0, 2):
        low, high = window(SIDE * s + y - 1), window(SIDE * (s + 1) + y - 1)
        both = jnp.where(lane < HALO, pltpu.roll(low, HALO, 1), high)
        start = jnp.where(
            lane < HALO, 128 * (SIDE * s + y) - HALO, 128 * (SIDE * (s + 1) + y) - 2 * HALO
        )
        at = (start + lane).astype(F32)
        halo.append(jnp.where(at < 0.0, -1.0, both))
        halo_at.append(at)
    seg = jnp.concatenate(own + halo, axis=1)
    at = jnp.concatenate(own_at + halo_at, axis=1)
    keys = seg.shape[1]
    tokens = SIDE * 128
    number = lax.broadcasted_iota(jnp.int32, (128, keys), 0).astype(F32)
    docs = spread_rows(seg_doc[...].astype(F32))
    docs = jnp.concatenate([docs] * (keys // 128), axis=1)
    doc = jnp.sum(jnp.where(number == seg, docs, 0.0), axis=0, keepdims=True)
    order = jnp.where(seg < 0.0, 65536.0 + at, doc * 2048.0 + at)
    tall, tall_seg = spread_rows(order), spread_rows(seg)
    key_rank, rank, pos = [], [], []
    for c in range(keys // 128):
        cut = slice(128 * c, 128 * (c + 1))
        less = tall < order[:, cut]
        key_rank.append(count(less))
        if c < SIDE:
            rank.append(count(less[:tokens]))
            pos.append(count(less & (tall_seg == seg[:, cut])))
    key_rank, rank, pos = [jnp.concatenate(v, axis=1) for v in (key_rank, rank, pos)]
    doc = doc[:, :tokens]
    low, high = jnp.zeros_like(doc), jnp.zeros_like(doc)
    for d in range(doc_lens.shape[0]):
        length = doc_lens[d].astype(F32)
        low = low + jnp.where(doc > d, length, 0.0)
        high = high + jnp.where(doc >= d, length, 0.0)
    mine = key_rank[:, :tokens]
    ranges = [low, high, mine - pos, mine + 1.0]
    coarse = [jnp.floor(v * (1.0 / 64.0)) for v in ranges]
    fine = [v - 64.0 * c for v, c in zip(ranges, coarse)]
    table = jnp.concatenate(coarse + fine + [rank] * 8, axis=0)
    return table, jnp.concatenate([key_rank] * 8, axis=0), pos


def gather_project(
    gain, hid_far, seg_ids_far, seg_doc_far, doc_lens_far, wq, wkv, pfx, wo,
    q_out, kv, pfx_all, wo_low, table, key_table,
    xs, wqs, wkvs, cos, sin, hid, seg_ids, seg_doc, doc_lens,
    send, recv, x_send, x_recv, halo_send, halo_recv, stay,
):
    x, core, z, y = place()
    here = lambda dx, dcore, dz, dy: device(
        x + dx, core if dcore == 0 else 1 - core, z + dz, y + dy
    )
    down = SIDE - 1
    stays = [
        pltpu.make_async_copy(src, dst, stay.at[k])
        for k, (src, dst) in enumerate(
            [
                (hid_far, hid),
                (seg_ids_far, seg_ids),
                (seg_doc_far, seg_doc),
                (doc_lens_far, doc_lens),
                (wkv, wkvs.at[y]),
                (wq, wqs.at[y]),
                (pfx, pfx_all.at[y]),
                (wo.at[:, pl.ds(0, wo_low.shape[2])], wo_low.at[y]),
            ]
        )
    ]
    for copy in stays:
        copy.start()
    greet([
        here(0, 0, 0, 1), here(0, 0, 0, down), here(0, 0, 1, 0), here(0, 0, down, 0),
        here(1, 0, 0, 0), here(down, 0, 0, 0), here(0, 1, 0, 0),
    ])

    def third(array, size):
        return lambda n: array.at[pl.ds(0, 3), pl.ds(0, n * size), :]

    parts = [
        pieces(wkv, wkvs, 512, 512) + (third(wkvs, 2048),),
        pieces(wq, wqs, 512, 256) + (third(wqs, 1024),),
        pieces(wq, wqs, 512, 256, 256) + (third(wqs, 1024),),
        pieces(pfx, pfx_all, 512, 512) + (third(pfx_all, 2048),),
        pieces(wo, wo_low, 32, 32, 0, (0, wo_low.shape[2])) + (third(wo_low, 128),),
    ]
    units = [Spread(*part, send.at[k], recv.at[k]) for k, part in enumerate(parts)]
    units[0].start()

    stays[0].wait()
    values = hid[...].astype(F32)
    scale = lax.rsqrt(jnp.mean(values * values, axis=-1, keepdims=True) + EPS)
    xs[z] = (values * scale * gain[...].astype(F32)).astype(BF16)

    per_half = HALO // PIECE

    def x_copy(side, n, d=0):
        view = xs.at[(z + d) % SIDE, pl.ds(PIECE * n, PIECE), :]
        i = n + (2 * per_half if d else 0)
        to = here(0, 0, down if side else 1, 0)
        return remote(view, view, x_send.at[side], x_recv.at[side, i], to)

    def first_half(side, k):
        return (k + per_half * side) % (2 * per_half)

    def x_own(k):
        if k < 2 * per_half:
            for side in range(2):
                x_copy(side, first_half(side, k)).start()

    def x_got(k):
        for side in range(2):
            d = 1 if side else down
            if k < 2 * per_half:
                n = first_half(side, k)
                view = xs.at[(z + d) % SIDE, pl.ds(PIECE * n, PIECE), :]
                i = n
            else:
                n = first_half(side, k - 2 * per_half)
                view = xs.at[(z + 2) % SIDE, pl.ds(PIECE * n, PIECE), :]
                i = n + 2 * per_half
            remote(view, view, x_send.at[side], x_recv.at[side, i], here(0, 0, 1, 0)).wait_recv()
            if k < per_half:
                x_copy(side, n, d).start()

    tokens = SIDE * 128
    half_rows = 2 * 128

    def project_kv():
        for s in range(SIDE):
            @pl.loop(0, 2)
            def _(m):
                tall = pl.ds(pl.multiple_of(m * half_rows, half_rows), half_rows)
                lhs = xs[pl.ds(2 * m, 2)].reshape(half_rows, xs.shape[2])
                got = jnp.dot(lhs, wkvs[s], preferred_element_type=F32)
                if s % 2 == 0:
                    got = rotate(got, cos[tall, :], sin[tall, :])
                kv[tall, pl.ds(HEAD * s, HEAD)] = got.astype(BF16)

    def project_q(s):
        @pl.loop(0, 2)
        def _(m):
            tall = pl.ds(pl.multiple_of(m * half_rows, half_rows), half_rows)
            lhs = xs[pl.ds(2 * m, 2)].reshape(half_rows, xs.shape[2])
            got = jnp.dot(lhs, wqs[s], preferred_element_type=F32)
            for n in range(2):
                one = rotate(got[:, HEAD * n : HEAD * (n + 1)], cos[tall, :], sin[tall, :])
                q_out[tall, pl.ds(HEAD * (2 * s + n), HEAD)] = one.astype(BF16)

    def halo_copy(slot):
        dst = (slot + y // 3) % SIDE
        return remote(
            kv.at[pl.ds(128 * slot + HALO, HALO), :],
            kv.at[pl.ds(pl.multiple_of(tokens + HALO * dst, HALO), HALO), :],
            halo_send.at[slot],
            halo_recv.at[slot],
            here(0, 0, 0, 1),
        )

    def describe_tokens():
        for k in range(1, 4):
            stays[k].wait()
        rows, key_rows, pos = describe(seg_ids, seg_doc, doc_lens, y)
        table[...] = rows
        key_table[...] = key_rows
        lane = lax.broadcasted_iota(jnp.int32, (1, HEAD), 1)
        inverse = jnp.zeros((1, HEAD), F32)
        for i in range(HEAD // 2):
            inverse = jnp.where(lane % (HEAD // 2) == i, THETA ** (-2.0 * i / HEAD), inverse)
        angle = (pfx.shape[0] + spread_rows(pos)) * inverse
        cos[...] = jnp.cos(angle)
        turn = jnp.sin(angle)
        sin[...] = jnp.where(lane < HEAD // 2, -turn, turn)

    def keys_and_values():
        for k in range(4, 6):
            stays[k].wait()
        for unit in units[:3]:
            unit.sibling()
        project_kv()
        for slot in range(SIDE):
            halo_copy(slot).start()

    extra = {3: describe_tokens, 13: keys_and_values}
    for s in range(SIDE):
        extra[14 + s] = functools.partial(project_q, s)
    lag = 2
    ahead = 8
    for k in range(ahead):
        x_own(k)
    for t in range(max(3 * len(units) + lag, 18)):
        if t < 3 * len(units):
            for i in Y_ROUNDS[t % 3]:
                units[t // 3].along_y(i)
            if t % 3 == 0 and t // 3 + 1 < len(units):
                units[t // 3 + 1].start()
        if 1 <= t < 3 * per_half + 1:
            x_got(t - 1)
            x_own(t - 1 + ahead)
        if lag <= t < 3 * len(units) + lag:
            for i in X_ROUNDS[(t - lag) % 3]:
                units[(t - lag) // 3].along_x(i)
        if t in extra:
            extra[t]()
    for unit in units[3:]:
        unit.sibling()
    for k in range(6, 8):
        stays[k].wait()
    for slot in range(SIDE):
        halo_copy(slot).wait()
    for side in range(2):
        view = xs.at[pl.ds(0, 3), pl.ds(0, HALO), :]
        remote(view, view, x_send.at[side], x_recv.at[side, 0], here(0, 0, 1, 0)).wait_send()
    for unit in units:
        unit.sent()


TILE = 128
NEW_KEYS = 256
PREFIX_KEYS = 512


def attend(
    table, key_table, q, kv, pfx, out,
    perm, qs, kvs, ranges, outs, top, acc, new_scores, prefix_scores,
):
    tokens, news, prefix = q.shape[0], kv.shape[0], pfx.shape[1]
    group = 4
    exponent = math.log2(math.e) / math.sqrt(HEAD)

    def one_hot(flags):
        return jnp.where(flags, 1.0, 0.0).astype(BF16)

    rank = table[8:9, :]
    spots = lax.broadcasted_iota(jnp.int32, (tokens, tokens), 0).astype(F32)
    by_doc = one_hot(spots == rank)
    qs[...] = jnp.dot(by_doc, q[...], preferred_element_type=F32).astype(BF16)
    got = lax.dot_general(
        by_doc, table[...].astype(BF16), (((1,), (1,)), ((), ())), preferred_element_type=F32
    )
    for k in range(4):
        column = 64.0 * got[:, k : k + 1] + got[:, k + 4 : k + 5]
        ranges[k] = jnp.broadcast_to(column, (tokens, 128)).astype(jnp.int32)
    spots = lax.broadcasted_iota(jnp.int32, (news, news), 0).astype(F32)
    kvs[...] = jnp.dot(
        one_hot(spots == key_table[0:1, :]), kv[...], preferred_element_type=F32
    ).astype(BF16)
    tall = spread_rows(rank)
    lane = lax.broadcasted_iota(jnp.int32, (tokens, 128), 1)
    for c in range(tokens // 128):
        perm[:, pl.ds(128 * c, 128)] = one_hot(tall == (lane + 128 * c).astype(F32))

    @pl.loop(0, tokens // TILE)
    def _(i):
        cut = pl.ds(pl.multiple_of(i * TILE, TILE), TILE)
        top[...] = jnp.full(top.shape, MASKED, F32)
        acc[...] = jnp.zeros(acc.shape, F32)
        queries = [
            jnp.concatenate(
                [qs[cut, pl.ds(HEAD * (group * h + n), HEAD)] for n in range(group)], axis=0
            )
            for h in range(2)
        ]

        def extent(kind, keys):
            first = jnp.min(ranges[kind, cut, :]) // 128 * 128
            last = jnp.max(ranges[kind + 1, cut, :])
            return first, (last - first + keys - 1) // keys

        def begin_at(first, j, keys, size):
            return pl.multiple_of(jnp.minimum(first + j * keys, size - keys), 128)

        def score(kind, where, keys, size, load, scores):
            first, steps = where

            @pl.loop(0, steps)
            def _(j):
                start = begin_at(first, j, keys, size)
                near = jnp.maximum(ranges[kind, cut, :], first + j * keys) - start
                far = ranges[kind + 1, cut, :] - start
                at = lax.broadcasted_iota(jnp.int32, (TILE, 128), 1)
                bias = jnp.concatenate(
                    [
                        jnp.where((at + c >= near) & (at + c < far), 0.0, MASKED)
                        for c in range(0, keys, 128)
                    ],
                    axis=1,
                )
                bias = jnp.concatenate([bias] * group, axis=0)
                for h in range(2):
                    s = bias + lax.dot_general(
                        queries[h],
                        load(2 * h, pl.ds(start, keys)),
                        (((1,), (1,)), ((), ())),
                        preferred_element_type=F32,
                    )
                    scores[h, j] = s
                    best = top[h]
                    for c in range(0, keys, 128):
                        best = jnp.maximum(best, s[:, c : c + 128])
                    top[h] = best

        def weigh(where, keys, size, load, scores):
            first, steps = where

            @pl.loop(0, steps)
            def _(j):
                start = begin_at(first, j, keys, size)
                for h in range(2):
                    best = jnp.concatenate([top[h]] * (keys // 128), axis=1)
                    p = jnp.exp2((scores[h, j] - best) * exponent).astype(BF16)
                    value = load(2 * h + 1, pl.ds(start, keys))
                    value = jnp.concatenate([value, jnp.ones_like(value)], axis=1)
                    acc[h] += jnp.dot(p, value, preferred_element_type=F32)

        load_new = lambda column, at: kvs[at, pl.ds(HEAD * column, HEAD)]
        load_prefix = lambda column, at: pfx[column, at, :]
        own, doc = extent(2, NEW_KEYS), extent(0, PREFIX_KEYS)
        score(2, own, NEW_KEYS, news, load_new, new_scores)
        score(0, doc, PREFIX_KEYS, prefix, load_prefix, prefix_scores)
        for h in range(2):
            best = jnp.max(top[h], axis=1, keepdims=True)
            top[h] = jnp.broadcast_to(best, top.shape[1:])
        weigh(own, NEW_KEYS, news, load_new, new_scores)
        weigh(doc, PREFIX_KEYS, prefix, load_prefix, prefix_scores)
        for h in range(2):
            done = (acc[h, :, pl.ds(0, HEAD)] / acc[h, :, pl.ds(HEAD, HEAD)]).astype(BF16)
            for n in range(group):
                outs[cut, pl.ds(HEAD * (group * h + n), HEAD)] = done[n * TILE : (n + 1) * TILE]

    out[...] = jnp.dot(perm[...], outs[...], preferred_element_type=F32).astype(BF16)


COLS = 512


def project_reduce(
    att, wo_low, wo, hid_far, mixed,
    wo_high, hid, far_out, near_out, far_in, near_in,
    far_send, far_recv, near_send, near_recv, send, recv, stay,
):
    x, core, z, y = place()
    down = SIDE - 1
    sides = [device(x, core, z + 1, y), device(x, core, z + down, y)]
    half = wo_low.shape[2]
    stays = [
        pltpu.make_async_copy(wo.at[:, pl.ds(half, half)], wo_high.at[y], stay.at[0]),
        pltpu.make_async_copy(hid_far, hid, stay.at[1]),
    ]
    for copy in stays:
        copy.start()
    greet(
        sides
        + [device(x, core, z, y + 1), device(x, core, z, y + down)]
        + [device(x + 1, core, z, y), device(x + down, core, z, y), device(x, 1 - core, z, y)]
    )
    bulk = lambda n: wo_high.at[pl.ds(0, 3), pl.ds(0, 128 * n), :]
    unit = Spread(*pieces(wo, wo_high, 32, 32, 0, (half, half)), bulk, send.at[0], recv.at[0])
    unit.start()
    chunks = 2 * half // COLS

    def partial(slot, j):
        source, at = (wo_low, j) if j < chunks // 2 else (wo_high, j - chunks // 2)
        weight = source[:, :, pl.ds(COLS * at, COLS)].reshape(-1, COLS)
        return jnp.dot(att[slot % SIDE], weight, preferred_element_type=F32)

    def far(j):
        return remote(far_out.at[j], far_in.at[j], far_send.at[j], far_recv.at[j], sides[j % 2])

    def near(side, j):
        return remote(
            near_out.at[side, j],
            near_in.at[side, j],
            near_send.at[side, j],
            near_recv.at[side, j],
            sides[side],
        )

    def far_step(j):
        far_out[j] = partial(z + 2, j).astype(BF16)
        far(j).start()

    def near_step(j):
        side = 1 - j % 2
        near_out[side, j] = partial(z + (down if side else 1), j).astype(BF16)
        near(side, j).start()
        side = j % 2
        mine = partial(z + (down if side else 1), j)
        far(j).wait_recv()
        near_out[side, j] = (mine + far_in[j].astype(F32)).astype(BF16)
        near(side, j).start()

    def along_y(r):
        for i in Y_ROUNDS[r]:
            unit.along_y(i)

    def along_x(r):
        for i in X_ROUNDS[r]:
            unit.along_x(i)

    for j in range(chunks // 2):
        far_step(j)
    along_y(0)
    near_step(0)
    near_step(1)
    along_y(1)
    along_x(0)
    near_step(2)
    along_y(2)
    along_x(1)
    near_step(3)
    along_x(2)
    stays[0].wait()
    unit.sibling()
    for j in range(chunks // 2, chunks):
        far_step(j)
    for j in range(chunks // 2, chunks):
        near_step(j)
    stays[1].wait()
    for j in range(chunks):
        cut = pl.ds(COLS * j, COLS)
        mine = partial(z, j) + hid[:, cut].astype(F32)
        near(0, j).wait_recv()
        near(1, j).wait_recv()
        mine = mine + near_in[0, j].astype(F32) + near_in[1, j].astype(F32)
        mixed[:, cut] = mine.astype(BF16)
    for j in range(chunks):
        far(j).wait_send()
        near(0, j).wait_send()
        near(1, j).wait_send()
    unit.sent()


def local(hidden_in, norm_gain, w_query, keyvalue_weight, w_out, cache, seg_ids, seg_doc, doc_lens):
    prefix_len = cache.shape[0]
    width = hidden_in.shape[1]
    half = width // 2
    far = lambda array: pltpu.with_memory_space_constraint(array, pltpu.HBM)
    vmem = pl.BlockSpec(memory_space=pltpu.VMEM)
    whole = pl.BlockSpec(memory_space=pltpu.HBM)
    tokens = SIDE * 128
    news = tokens + SIDE * HALO
    q, kv, pfx, wo_low, table, key_table = pl.pallas_call(
        gather_project,
        out_shape=(
            jax.ShapeDtypeStruct((tokens, 8 * HEAD), BF16),
            jax.ShapeDtypeStruct((news, 4 * HEAD), BF16),
            jax.ShapeDtypeStruct((SIDE, prefix_len, HEAD), BF16),
            jax.ShapeDtypeStruct((SIDE, w_out.shape[0], half), BF16),
            jax.ShapeDtypeStruct((16, tokens), F32),
            jax.ShapeDtypeStruct((8, news), F32),
        ),
        in_specs=[vmem] + [whole] * 8,
        out_specs=(vmem,) * 6,
        scratch_shapes=[
            pltpu.VMEM((SIDE, 128, width), BF16),
            pltpu.VMEM((SIDE,) + w_query.shape, BF16),
            pltpu.VMEM((SIDE,) + keyvalue_weight.shape, BF16),
            pltpu.VMEM((tokens, HEAD), F32),
            pltpu.VMEM((tokens, HEAD), F32),
            pltpu.VMEM(hidden_in.shape, BF16),
            pltpu.VMEM((1,) + seg_ids.shape, jnp.int32),
            pltpu.VMEM((1,) + seg_doc.shape, jnp.int32),
            pltpu.SMEM(doc_lens.shape, jnp.int32),
            pltpu.SemaphoreType.DMA((5,)),
            pltpu.SemaphoreType.DMA((5, 13)),
            pltpu.SemaphoreType.DMA((2,)),
            pltpu.SemaphoreType.DMA((2, 16)),
            pltpu.SemaphoreType.DMA((4,)),
            pltpu.SemaphoreType.DMA((4,)),
            pltpu.SemaphoreType.DMA((8,)),
        ],
        compiler_params=pltpu.CompilerParams(
            collective_id=0, has_side_effects=True, vmem_limit_bytes=30 * 2**20
        ),
        name="gather_project",
    )(
        norm_gain[None, :],
        far(hidden_in),
        far(seg_ids[None, :]),
        far(seg_doc[None, :]),
        far(doc_lens),
        far(w_query),
        far(keyvalue_weight),
        far(cache),
        far(w_out),
    )

    attended = pl.pallas_call(
        attend,
        out_shape=jax.ShapeDtypeStruct((tokens, 8 * HEAD), BF16),
        in_specs=[vmem] * 5,
        out_specs=vmem,
        scratch_shapes=[
            pltpu.VMEM((tokens, tokens), BF16),
            pltpu.VMEM((tokens, 8 * HEAD), BF16),
            pltpu.VMEM((news, 4 * HEAD), BF16),
            pltpu.VMEM((4, tokens, 128), jnp.int32),
            pltpu.VMEM((tokens, 8 * HEAD), BF16),
            pltpu.VMEM((2, 4 * TILE, 128), F32),
            pltpu.VMEM((2, 4 * TILE, 2 * HEAD), F32),
            pltpu.VMEM((2, news // NEW_KEYS, 4 * TILE, NEW_KEYS), F32),
            pltpu.VMEM((2, prefix_len // PREFIX_KEYS, 4 * TILE, PREFIX_KEYS), F32),
        ],
        compiler_params=pltpu.CompilerParams(vmem_limit_bytes=40 * 2**20),
        name="attend",
    )(table, key_table, q, kv, pfx)

    chunks = width // COLS
    return pl.pallas_call(
        project_reduce,
        out_shape=jax.ShapeDtypeStruct(hidden_in.shape, BF16),
        in_specs=[vmem] * 2 + [whole] * 2,
        out_specs=vmem,
        scratch_shapes=[
            pltpu.VMEM((SIDE, w_out.shape[0], half), BF16),
            pltpu.VMEM(hidden_in.shape, BF16),
            pltpu.VMEM((chunks, 128, COLS), BF16),
            pltpu.VMEM((2, chunks, 128, COLS), BF16),
            pltpu.VMEM((chunks, 128, COLS), BF16),
            pltpu.VMEM((2, chunks, 128, COLS), BF16),
            pltpu.SemaphoreType.DMA((chunks,)),
            pltpu.SemaphoreType.DMA((chunks,)),
            pltpu.SemaphoreType.DMA((2, chunks)),
            pltpu.SemaphoreType.DMA((2, chunks)),
            pltpu.SemaphoreType.DMA((1,)),
            pltpu.SemaphoreType.DMA((1, 13)),
            pltpu.SemaphoreType.DMA((2,)),
        ],
        compiler_params=pltpu.CompilerParams(
            collective_id=1, has_side_effects=True, vmem_limit_bytes=32 * 2**20
        ),
        name="project_reduce",
    )(attended.reshape(SIDE, 128, 8 * HEAD), wo_low, far(w_out), far(hidden_in))


def solution(mesh):
    return jax.shard_map(
        local,
        mesh=mesh,
        in_specs=(
            P(("dp", "tensor"), None),
            P(),
            P(None, "tensor"),
            P(None, "tensor"),
            P("tensor", None),
            P(None, "tensor"),
            P("dp"),
            P("dp"),
            P(),
        ),
        out_specs=P(("dp", "tensor"), None),
        check_vma=False,
    )
```

```python
import functools
import math

import jax
import jax.numpy as jnp
from jax import lax
from jax.experimental import pallas as pl
from jax.experimental.pallas import tpu as pltpu
from jax.sharding import PartitionSpec as P

HEAD = 128
HALO = 64
SIDE = 4
EPS = 1e-05
THETA = 500000.0
MASKED = -1e30
MESH = pl.DeviceIdType.MESH
BF16 = jnp.bfloat16
F32 = jnp.float32


def place():
    dp, tensor = lax.axis_index("dp"), lax.axis_index("tensor")
    return dp // 2, dp % 2, tensor // SIDE, tensor % SIDE


def device(x, core, z, y):
    return (2 * (x % SIDE) + core, SIDE * (z % SIDE) + y % SIDE)


def greet(others):
    barrier = pltpu.get_barrier_semaphore()
    for other in others:
        pl.semaphore_signal(barrier, inc=1, device_id=other, device_id_type=MESH)
    pl.semaphore_wait(barrier, len(others))


def remote(src, dst, send, recv, other):
    return pltpu.make_async_remote_copy(
        src_ref=src, dst_ref=dst, send_sem=send, recv_sem=recv, device_id=other, device_id_type=MESH
    )


def rotate(v, cos, sin):
    return v * cos + pltpu.roll(v, HEAD // 2, 1) * sin


def pieces(own, every, step, size, offset=0, cols=None):
    across = slice(None) if cols is None else pl.ds(*cols)

    def at(n):
        return pl.ds(pl.multiple_of(n * step + offset, size), size)

    return lambda n: own.at[at(n), across], lambda s, n: every.at[s, at(n), :]


class Spread:
    def __init__(self, own, block, bulk, send, recv):
        self.own, self.block, self.bulk, self.send, self.recv = own, block, bulk, send, recv
        self.x, self.core, self.z, self.y = place()

    def number(self, parity, core, half):
        return 4 * parity + 2 * core + half

    def up(self, n):
        return (self.x, self.core, self.z, self.y + n)

    def copy(self, i, d, piece, to, first=False):
        slot = (self.y + d + SIDE) % SIDE
        src = self.own(piece) if first else self.block(slot, piece)
        return remote(
            src, self.block(slot, piece), self.send, self.recv.at[min(i, 12)], device(*to)
        )

    def mine(self, half):
        return self.number(self.x % 2, self.core, half)

    def sends(self, i):
        if i in (0, 1):
            return self.copy(i, 0, self.mine(i), self.up(1), True)
        if i == 2:
            return self.copy(i, 3, self.mine(0), self.up(1))
        if i in (3, 4):
            return self.copy(i, 0, self.mine(4 - i), self.up(SIDE - 1), True)
        if i == 5:
            return self.copy(i, 1, self.mine(1), self.up(SIDE - 1))
        d, half = 1 + (i % 6) // 2, i % 2
        if i < 12:
            to = (self.x + (SIDE - 1 if half else 1), self.core, self.z, self.y)
            return self.copy(i, d, self.mine(half), to)
        parity = self.x % 2 if i < 18 else 1 - self.x % 2
        piece = self.number(parity, self.core, half)
        return self.copy(i, d, piece, (self.x, 1 - self.core, self.z, self.y))

    def got(self, i):
        if i < 6:
            d = {0: 3, 1: 3, 2: 2, 3: 1, 4: 1, 5: 2}[i]
            half = {0: 0, 1: 1, 2: 0, 3: 1, 4: 0, 5: 1}[i]
            piece = self.mine(half)
        else:
            d, half = 1 + (i % 6) // 2, i % 2
            piece = self.number(1 - self.x % 2, self.core, half)
        view = self.block((self.y + d) % SIDE, piece)
        remote(view, view, self.send, self.recv.at[i], device(*self.up(1))).wait_recv()

    def start(self):
        for i in (0, 3, 1, 4):
            self.sends(i).start()

    def along_y(self, i):
        self.got(i)
        if i == 0:
            self.sends(2).start()
        if i == 3:
            self.sends(5).start()
        d = {0: 3, 1: 3, 2: 2, 3: 1, 4: 1, 5: 2}[i]
        half = {0: 0, 1: 1, 2: 0, 3: 1, 4: 0, 5: 1}[i]
        self.sends(6 + 2 * (d - 1) + half).start()
        self.sends(12 + 2 * (d - 1) + half).start()

    def along_x(self, i):
        self.got(i)
        self.sends(i + 12).start()

    def sibling(self):
        view = self.bulk(1)
        remote(view, view, self.send, self.recv.at[12], device(*self.up(1))).wait_recv()

    def sent(self):
        view = self.bulk(2)
        remote(view, view, self.send, self.recv.at[12], device(*self.up(1))).wait_send()


Y_ROUNDS = ((0, 3), (1, 4), (2, 5))
X_ROUNDS = ((10, 7), (11, 6), (8, 9))
PIECE = 16


def spread_rows(row):
    return jnp.transpose(jnp.broadcast_to(row, (128, row.shape[1])))


def count(flags):
    return jnp.sum(jnp.where(flags, 1.0, 0.0), axis=0, keepdims=True)


def describe(seg_ids, seg_doc, doc_lens, y):
    lane = lax.broadcasted_iota(jnp.int32, (1, 128), 1)

    def window(n):
        return seg_ids[:, pl.ds(pl.multiple_of(128 * jnp.maximum(n, 0), 128), 128)].astype(F32)

    own = [window(SIDE * s + y) for s in range(SIDE)]
    own_at = [(128 * (SIDE * s + y) + lane).astype(F32) for s in range(SIDE)]
    halo, halo_at = [], []
    for s in (0, 2):
        low, high = window(SIDE * s + y - 1), window(SIDE * (s + 1) + y - 1)
        both = jnp.where(lane < HALO, pltpu.roll(low, HALO, 1), high)
        start = jnp.where(
            lane < HALO, 128 * (SIDE * s + y) - HALO, 128 * (SIDE * (s + 1) + y) - 2 * HALO
        )
        at = (start + lane).astype(F32)
        halo.append(jnp.where(at < 0.0, -1.0, both))
        halo_at.append(at)
    seg = jnp.concatenate(own + halo, axis=1)
    at = jnp.concatenate(own_at + halo_at, axis=1)
    keys = seg.shape[1]
    tokens = SIDE * 128
    number = lax.broadcasted_iota(jnp.int32, (128, keys), 0).astype(F32)
    docs = spread_rows(seg_doc[...].astype(F32))
    docs = jnp.concatenate([docs] * (keys // 128), axis=1)
    doc = jnp.sum(jnp.where(number == seg, docs, 0.0), axis=0, keepdims=True)
    order = jnp.where(seg < 0.0, 65536.0 + at, doc * 2048.0 + at)
    tall, tall_seg = spread_rows(order), spread_rows(seg)
    key_rank, rank, pos = [], [], []
    for c in range(keys // 128):
        cut = slice(128 * c, 128 * (c + 1))
        less = tall < order[:, cut]
        key_rank.append(count(less))
        if c < SIDE:
            rank.append(count(less[:tokens]))
            pos.append(count(less & (tall_seg == seg[:, cut])))
    key_rank, rank, pos = [jnp.concatenate(v, axis=1) for v in (key_rank, rank, pos)]
    doc = doc[:, :tokens]
    low, high = jnp.zeros_like(doc), jnp.zeros_like(doc)
    for d in range(doc_lens.shape[0]):
        length = doc_lens[d].astype(F32)
        low = low + jnp.where(doc > d, length, 0.0)
        high = high + jnp.where(doc >= d, length, 0.0)
    mine = key_rank[:, :tokens]
    ranges = [low, high, mine - pos, mine + 1.0]
    coarse = [jnp.floor(v * (1.0 / 64.0)) for v in ranges]
    fine = [v - 64.0 * c for v, c in zip(ranges, coarse)]
    table = jnp.concatenate(coarse + fine + [rank] * 8, axis=0)
    return table, jnp.concatenate([key_rank] * 8, axis=0), pos


def gather_project(
    gain, hid_far, seg_ids_far, seg_doc_far, doc_lens_far, wq, wkv, pfx, wo,
    q_out, kv, pfx_all, wo_low, table, key_table,
    xs, wqs, wkvs, cos, sin, hid, seg_ids, seg_doc, doc_lens,
    send, recv, x_send, x_recv, halo_send, halo_recv, stay,
):
    x, core, z, y = place()
    here = lambda dx, dcore, dz, dy: device(
        x + dx, core if dcore == 0 else 1 - core, z + dz, y + dy
    )
    down = SIDE - 1
    stays = [
        pltpu.make_async_copy(src, dst, stay.at[k])
        for k, (src, dst) in enumerate(
            [
                (hid_far, hid),
                (seg_ids_far, seg_ids),
                (seg_doc_far, seg_doc),
                (doc_lens_far, doc_lens),
                (wkv, wkvs.at[y]),
                (wq, wqs.at[y]),
                (pfx, pfx_all.at[y]),
                (wo.at[:, pl.ds(0, wo_low.shape[2])], wo_low.at[y]),
            ]
        )
    ]
    for copy in stays:
        copy.start()
    greet([
        here(0, 0, 0, 1), here(0, 0, 0, down), here(0, 0, 1, 0), here(0, 0, down, 0),
        here(1, 0, 0, 0), here(down, 0, 0, 0), here(0, 1, 0, 0),
    ])

    def third(array, size):
        return lambda n: array.at[pl.ds(0, 3), pl.ds(0, n * size), :]

    parts = [
        pieces(wkv, wkvs, 512, 512) + (third(wkvs, 2048),),
        pieces(wq, wqs, 512, 256) + (third(wqs, 1024),),
        pieces(wq, wqs, 512, 256, 256) + (third(wqs, 1024),),
        pieces(pfx, pfx_all, 512, 512) + (third(pfx_all, 2048),),
        pieces(wo, wo_low, 32, 32, 0, (0, wo_low.shape[2])) + (third(wo_low, 128),),
    ]
    units = [Spread(*part, send.at[k], recv.at[k]) for k, part in enumerate(parts)]
    units[0].start()

    stays[0].wait()
    values = hid[...].astype(F32)
    scale = lax.rsqrt(jnp.mean(values * values, axis=-1, keepdims=True) + EPS)
    xs[z] = (values * scale * gain[...].astype(F32)).astype(BF16)

    per_half = HALO // PIECE

    def x_copy(side, n, d=0):
        view = xs.at[(z + d) % SIDE, pl.ds(PIECE * n, PIECE), :]
        i = n + (2 * per_half if d else 0)
        to = here(0, 0, down if side else 1, 0)
        return remote(view, view, x_send.at[side], x_recv.at[side, i], to)

    def first_half(side, k):
        return (k + per_half * side) % (2 * per_half)

    def x_own(k):
        if k < 2 * per_half:
            for side in range(2):
                x_copy(side, first_half(side, k)).start()

    def x_got(k):
        for side in range(2):
            d = 1 if side else down
            if k < 2 * per_half:
                n = first_half(side, k)
                view = xs.at[(z + d) % SIDE, pl.ds(PIECE * n, PIECE), :]
                i = n
            else:
                n = first_half(side, k - 2 * per_half)
                view = xs.at[(z + 2) % SIDE, pl.ds(PIECE * n, PIECE), :]
                i = n + 2 * per_half
            remote(view, view, x_send.at[side], x_recv.at[side, i], here(0, 0, 1, 0)).wait_recv()
            if k < per_half:
                x_copy(side, n, d).start()

    tokens = SIDE * 128
    def both(ds):
        return jnp.concatenate([xs[(z + d) % SIDE] for d in ds], axis=0)

    def group(d):
        return pl.ds(pl.multiple_of((z + d) % SIDE * 128, 128), 128)

    def project_kv(ds):
        for h in range(2):
            weight = jnp.concatenate([wkvs[2 * h], wkvs[2 * h + 1]], axis=1)
            got = jnp.dot(both(ds), weight, preferred_element_type=F32)
            for n, d in enumerate(ds):
                part, at = got[128 * n : 128 * (n + 1)], group(d)
                key = rotate(part[:, :HEAD], cos[at, :], sin[at, :])
                kv[at, pl.ds(2 * HEAD * h, HEAD)] = key.astype(BF16)
                kv[at, pl.ds(2 * HEAD * h + HEAD, HEAD)] = part[:, HEAD:].astype(BF16)

    def project_q(ds, s):
        got = jnp.dot(both(ds), wqs[s], preferred_element_type=F32)
        for n, d in enumerate(ds):
            part, at = got[128 * n : 128 * (n + 1)], group(d)
            for m in range(2):
                one = rotate(part[:, HEAD * m : HEAD * (m + 1)], cos[at, :], sin[at, :])
                q_out[at, pl.ds(HEAD * (2 * s + m), HEAD)] = one.astype(BF16)

    def halo_copy(slot):
        dst = (slot + y // 3) % SIDE
        return remote(
            kv.at[pl.ds(128 * slot + HALO, HALO), :],
            kv.at[pl.ds(pl.multiple_of(tokens + HALO * dst, HALO), HALO), :],
            halo_send.at[slot],
            halo_recv.at[slot],
            here(0, 0, 0, 1),
        )

    def describe_tokens():
        for k in range(1, 4):
            stays[k].wait()
        rows, key_rows, pos = describe(seg_ids, seg_doc, doc_lens, y)
        table[...] = rows
        key_table[...] = key_rows
        lane = lax.broadcasted_iota(jnp.int32, (1, HEAD), 1)
        inverse = jnp.zeros((1, HEAD), F32)
        for i in range(HEAD // 2):
            inverse = jnp.where(lane % (HEAD // 2) == i, THETA ** (-2.0 * i / HEAD), inverse)
        angle = (pfx.shape[0] + spread_rows(pos)) * inverse
        cos[...] = jnp.cos(angle)
        turn = jnp.sin(angle)
        sin[...] = jnp.where(lane < HEAD // 2, -turn, turn)

    early, late = (0, 1), (3, 2)

    def early_kv():
        stays[4].wait()
        units[0].sibling()
        project_kv(early)

    def early_q():
        stays[5].wait()
        for unit in units[1:3]:
            unit.sibling()
        project_q(early, 0)
        project_q(early, 1)

    def late_kv():
        project_kv(late)
        for slot in range(SIDE):
            halo_copy(slot).start()

    extra = {
        3: [describe_tokens],
        9: [early_kv],
        11: [early_q],
        12: [lambda: project_q(early, 2), lambda: project_q(early, 3)],
        13: [late_kv],
        14: [lambda: project_q(late, 0), lambda: project_q(late, 1)],
        15: [lambda: project_q(late, 2), lambda: project_q(late, 3)],
    }
    lag = 2
    ahead = 8
    for k in range(ahead):
        x_own(k)
    for t in range(max(3 * len(units) + lag, 18)):
        if t < 3 * len(units):
            for i in Y_ROUNDS[t % 3]:
                units[t // 3].along_y(i)
            if t % 3 == 0 and t // 3 + 1 < len(units):
                units[t // 3 + 1].start()
        if 1 <= t < 3 * per_half + 1:
            x_got(t - 1)
            x_own(t - 1 + ahead)
        if lag <= t < 3 * len(units) + lag:
            for i in X_ROUNDS[(t - lag) % 3]:
                units[(t - lag) // 3].along_x(i)
        for work in extra.get(t, []):
            work()
    for unit in units[3:]:
        unit.sibling()
    for k in range(6, 8):
        stays[k].wait()
    for slot in range(SIDE):
        halo_copy(slot).wait()
    for side in range(2):
        view = xs.at[pl.ds(0, 3), pl.ds(0, HALO), :]
        remote(view, view, x_send.at[side], x_recv.at[side, 0], here(0, 0, 1, 0)).wait_send()
    for unit in units:
        unit.sent()


TILE = 128
NEW_KEYS = 256
PREFIX_KEYS = 512


def attend(
    table, key_table, q, kv, pfx, out,
    perm, qs, kvs, ranges, outs, top, acc, new_scores, prefix_scores,
):
    tokens, news, prefix = q.shape[0], kv.shape[0], pfx.shape[1]
    group = 4
    exponent = math.log2(math.e) / math.sqrt(HEAD)

    def one_hot(flags):
        return jnp.where(flags, 1.0, 0.0).astype(BF16)

    rank = table[8:9, :]
    spots = lax.broadcasted_iota(jnp.int32, (tokens, tokens), 0).astype(F32)
    by_doc = one_hot(spots == rank)
    qs[...] = jnp.dot(by_doc, q[...], preferred_element_type=F32).astype(BF16)
    got = lax.dot_general(
        by_doc, table[...].astype(BF16), (((1,), (1,)), ((), ())), preferred_element_type=F32
    )
    for k in range(4):
        column = 64.0 * got[:, k : k + 1] + got[:, k + 4 : k + 5]
        ranges[k] = jnp.broadcast_to(column, (tokens, 128)).astype(jnp.int32)
    spots = lax.broadcasted_iota(jnp.int32, (news, news), 0).astype(F32)
    kvs[...] = jnp.dot(
        one_hot(spots == key_table[0:1, :]), kv[...], preferred_element_type=F32
    ).astype(BF16)
    tall = spread_rows(rank)
    lane = lax.broadcasted_iota(jnp.int32, (tokens, 128), 1)
    for c in range(tokens // 128):
        perm[:, pl.ds(128 * c, 128)] = one_hot(tall == (lane + 128 * c).astype(F32))

    @pl.loop(0, tokens // TILE)
    def _(i):
        cut = pl.ds(pl.multiple_of(i * TILE, TILE), TILE)
        top[...] = jnp.full(top.shape, MASKED, F32)
        acc[...] = jnp.zeros(acc.shape, F32)
        queries = [
            jnp.concatenate(
                [qs[cut, pl.ds(HEAD * (group * h + n), HEAD)] for n in range(group)], axis=0
            )
            for h in range(2)
        ]

        def extent(kind, keys):
            first = jnp.min(ranges[kind, cut, :]) // 128 * 128
            last = jnp.max(ranges[kind + 1, cut, :])
            return first, (last - first + keys - 1) // keys

        def begin_at(first, j, keys, size):
            return pl.multiple_of(jnp.minimum(first + j * keys, size - keys), 128)

        def score(kind, where, keys, size, load, scores):
            first, steps = where

            @pl.loop(0, steps)
            def _(j):
                start = begin_at(first, j, keys, size)
                near = jnp.maximum(ranges[kind, cut, :], first + j * keys) - start
                far = ranges[kind + 1, cut, :] - start
                at = lax.broadcasted_iota(jnp.int32, (TILE, 128), 1)
                bias = jnp.concatenate(
                    [
                        jnp.where((at + c >= near) & (at + c < far), 0.0, MASKED)
                        for c in range(0, keys, 128)
                    ],
                    axis=1,
                )
                bias = jnp.concatenate([bias] * group, axis=0)
                for h in range(2):
                    s = bias + lax.dot_general(
                        queries[h],
                        load(2 * h, pl.ds(start, keys)),
                        (((1,), (1,)), ((), ())),
                        preferred_element_type=F32,
                    )
                    scores[h, j] = s
                    best = top[h]
                    for c in range(0, keys, 128):
                        best = jnp.maximum(best, s[:, c : c + 128])
                    top[h] = best

        def weigh(where, keys, size, load, scores):
            first, steps = where

            @pl.loop(0, steps)
            def _(j):
                start = begin_at(first, j, keys, size)
                for h in range(2):
                    best = jnp.concatenate([top[h]] * (keys // 128), axis=1)
                    p = jnp.exp2((scores[h, j] - best) * exponent).astype(BF16)
                    value = load(2 * h + 1, pl.ds(start, keys))
                    value = jnp.concatenate([value, jnp.ones_like(value)], axis=1)
                    acc[h] += jnp.dot(p, value, preferred_element_type=F32)

        load_new = lambda column, at: kvs[at, pl.ds(HEAD * column, HEAD)]
        load_prefix = lambda column, at: pfx[column, at, :]
        own, doc = extent(2, NEW_KEYS), extent(0, PREFIX_KEYS)
        score(2, own, NEW_KEYS, news, load_new, new_scores)
        score(0, doc, PREFIX_KEYS, prefix, load_prefix, prefix_scores)
        for h in range(2):
            best = jnp.max(top[h], axis=1, keepdims=True)
            top[h] = jnp.broadcast_to(best, top.shape[1:])
        weigh(own, NEW_KEYS, news, load_new, new_scores)
        weigh(doc, PREFIX_KEYS, prefix, load_prefix, prefix_scores)
        for h in range(2):
            done = (acc[h, :, pl.ds(0, HEAD)] / acc[h, :, pl.ds(HEAD, HEAD)]).astype(BF16)
            for n in range(group):
                outs[cut, pl.ds(HEAD * (group * h + n), HEAD)] = done[n * TILE : (n + 1) * TILE]

    out[...] = jnp.dot(perm[...], outs[...], preferred_element_type=F32).astype(BF16)


COLS = 512


def project_reduce(
    att, wo_low, wo, hid_far, mixed,
    wo_high, hid, far_out, near_out, far_in, near_in,
    far_send, far_recv, near_send, near_recv, send, recv, stay,
):
    x, core, z, y = place()
    down = SIDE - 1
    sides = [device(x, core, z + 1, y), device(x, core, z + down, y)]
    half = wo_low.shape[2]
    stays = [
        pltpu.make_async_copy(wo.at[:, pl.ds(half, half)], wo_high.at[y], stay.at[0]),
        pltpu.make_async_copy(hid_far, hid, stay.at[1]),
    ]
    for copy in stays:
        copy.start()
    greet(
        sides
        + [device(x, core, z, y + 1), device(x, core, z, y + down)]
        + [device(x + 1, core, z, y), device(x + down, core, z, y), device(x, 1 - core, z, y)]
    )
    bulk = lambda n: wo_high.at[pl.ds(0, 3), pl.ds(0, 128 * n), :]
    unit = Spread(*pieces(wo, wo_high, 32, 32, 0, (half, half)), bulk, send.at[0], recv.at[0])
    unit.start()
    chunks = 2 * half // COLS

    def partial(slot, j):
        source, at = (wo_low, j) if j < chunks // 2 else (wo_high, j - chunks // 2)
        weight = source[:, :, pl.ds(COLS * at, COLS)].reshape(-1, COLS)
        return jnp.dot(att[slot % SIDE], weight, preferred_element_type=F32)

    def far(j):
        return remote(far_out.at[j], far_in.at[j], far_send.at[j], far_recv.at[j], sides[j % 2])

    def near(side, j):
        return remote(
            near_out.at[side, j],
            near_in.at[side, j],
            near_send.at[side, j],
            near_recv.at[side, j],
            sides[side],
        )

    def far_step(j):
        far_out[j] = partial(z + 2, j).astype(BF16)
        far(j).start()

    def near_step(j):
        side = 1 - j % 2
        near_out[side, j] = partial(z + (down if side else 1), j).astype(BF16)
        near(side, j).start()
        side = j % 2
        mine = partial(z + (down if side else 1), j)
        far(j).wait_recv()
        near_out[side, j] = (mine + far_in[j].astype(F32)).astype(BF16)
        near(side, j).start()

    def along_y(r):
        for i in Y_ROUNDS[r]:
            unit.along_y(i)

    def along_x(r):
        for i in X_ROUNDS[r]:
            unit.along_x(i)

    for j in range(chunks // 2):
        far_step(j)
    along_y(0)
    near_step(0)
    near_step(1)
    along_y(1)
    along_x(0)
    near_step(2)
    along_y(2)
    along_x(1)
    near_step(3)
    along_x(2)
    stays[0].wait()
    unit.sibling()
    for j in range(chunks // 2, chunks):
        far_step(j)
    for j in range(chunks // 2, chunks):
        near_step(j)
    stays[1].wait()
    for j in range(chunks):
        cut = pl.ds(COLS * j, COLS)
        mine = partial(z, j) + hid[:, cut].astype(F32)
        near(0, j).wait_recv()
        near(1, j).wait_recv()
        mine = mine + near_in[0, j].astype(F32) + near_in[1, j].astype(F32)
        mixed[:, cut] = mine.astype(BF16)
    for j in range(chunks):
        far(j).wait_send()
        near(0, j).wait_send()
        near(1, j).wait_send()
    unit.sent()


def local(hidden_in, norm_gain, w_query, keyvalue_weight, w_out, cache, seg_ids, seg_doc, doc_lens):
    prefix_len = cache.shape[0]
    width = hidden_in.shape[1]
    half = width // 2
    far = lambda array: pltpu.with_memory_space_constraint(array, pltpu.HBM)
    vmem = pl.BlockSpec(memory_space=pltpu.VMEM)
    whole = pl.BlockSpec(memory_space=pltpu.HBM)
    tokens = SIDE * 128
    news = tokens + SIDE * HALO
    q, kv, pfx, wo_low, table, key_table = pl.pallas_call(
        gather_project,
        out_shape=(
            jax.ShapeDtypeStruct((tokens, 8 * HEAD), BF16),
            jax.ShapeDtypeStruct((news, 4 * HEAD), BF16),
            jax.ShapeDtypeStruct((SIDE, prefix_len, HEAD), BF16),
            jax.ShapeDtypeStruct((SIDE, w_out.shape[0], half), BF16),
            jax.ShapeDtypeStruct((16, tokens), F32),
            jax.ShapeDtypeStruct((8, news), F32),
        ),
        in_specs=[vmem] + [whole] * 8,
        out_specs=(vmem,) * 6,
        scratch_shapes=[
            pltpu.VMEM((SIDE, 128, width), BF16),
            pltpu.VMEM((SIDE,) + w_query.shape, BF16),
            pltpu.VMEM((SIDE,) + keyvalue_weight.shape, BF16),
            pltpu.VMEM((tokens, HEAD), F32),
            pltpu.VMEM((tokens, HEAD), F32),
            pltpu.VMEM(hidden_in.shape, BF16),
            pltpu.VMEM((1,) + seg_ids.shape, jnp.int32),
            pltpu.VMEM((1,) + seg_doc.shape, jnp.int32),
            pltpu.SMEM(doc_lens.shape, jnp.int32),
            pltpu.SemaphoreType.DMA((5,)),
            pltpu.SemaphoreType.DMA((5, 13)),
            pltpu.SemaphoreType.DMA((2,)),
            pltpu.SemaphoreType.DMA((2, 16)),
            pltpu.SemaphoreType.DMA((4,)),
            pltpu.SemaphoreType.DMA((4,)),
            pltpu.SemaphoreType.DMA((8,)),
        ],
        compiler_params=pltpu.CompilerParams(
            collective_id=0, has_side_effects=True, vmem_limit_bytes=30 * 2**20
        ),
        name="gather_project",
    )(
        norm_gain[None, :],
        far(hidden_in),
        far(seg_ids[None, :]),
        far(seg_doc[None, :]),
        far(doc_lens),
        far(w_query),
        far(keyvalue_weight),
        far(cache),
        far(w_out),
    )

    attended = pl.pallas_call(
        attend,
        out_shape=jax.ShapeDtypeStruct((tokens, 8 * HEAD), BF16),
        in_specs=[vmem] * 5,
        out_specs=vmem,
        scratch_shapes=[
            pltpu.VMEM((tokens, tokens), BF16),
            pltpu.VMEM((tokens, 8 * HEAD), BF16),
            pltpu.VMEM((news, 4 * HEAD), BF16),
            pltpu.VMEM((4, tokens, 128), jnp.int32),
            pltpu.VMEM((tokens, 8 * HEAD), BF16),
            pltpu.VMEM((2, 4 * TILE, 128), F32),
            pltpu.VMEM((2, 4 * TILE, 2 * HEAD), F32),
            pltpu.VMEM((2, news // NEW_KEYS, 4 * TILE, NEW_KEYS), F32),
            pltpu.VMEM((2, prefix_len // PREFIX_KEYS, 4 * TILE, PREFIX_KEYS), F32),
        ],
        compiler_params=pltpu.CompilerParams(vmem_limit_bytes=40 * 2**20),
        name="attend",
    )(table, key_table, q, kv, pfx)

    chunks = width // COLS
    return pl.pallas_call(
        project_reduce,
        out_shape=jax.ShapeDtypeStruct(hidden_in.shape, BF16),
        in_specs=[vmem] * 2 + [whole] * 2,
        out_specs=vmem,
        scratch_shapes=[
            pltpu.VMEM((SIDE, w_out.shape[0], half), BF16),
            pltpu.VMEM(hidden_in.shape, BF16),
            pltpu.VMEM((chunks, 128, COLS), BF16),
            pltpu.VMEM((2, chunks, 128, COLS), BF16),
            pltpu.VMEM((chunks, 128, COLS), BF16),
            pltpu.VMEM((2, chunks, 128, COLS), BF16),
            pltpu.SemaphoreType.DMA((chunks,)),
            pltpu.SemaphoreType.DMA((chunks,)),
            pltpu.SemaphoreType.DMA((2, chunks)),
            pltpu.SemaphoreType.DMA((2, chunks)),
            pltpu.SemaphoreType.DMA((1,)),
            pltpu.SemaphoreType.DMA((1, 13)),
            pltpu.SemaphoreType.DMA((2,)),
        ],
        compiler_params=pltpu.CompilerParams(
            collective_id=1, has_side_effects=True, vmem_limit_bytes=32 * 2**20
        ),
        name="project_reduce",
    )(attended.reshape(SIDE, 128, 8 * HEAD), wo_low, far(w_out), far(hidden_in))


def solution(mesh):
    return jax.shard_map(
        local,
        mesh=mesh,
        in_specs=(
            P(("dp", "tensor"), None),
            P(),
            P(None, "tensor"),
            P(None, "tensor"),
            P("tensor", None),
            P(None, "tensor"),
            P("dp"),
            P("dp"),
            P(),
        ),
        out_specs=P(("dp", "tensor"), None),
        check_vma=False,
    )
```

```python
import functools
import math

import jax
import jax.numpy as jnp
from jax import lax
from jax.experimental import pallas as pl
from jax.experimental.pallas import tpu as pltpu
from jax.sharding import PartitionSpec as P

HEAD = 128
HALO = 64
SIDE = 4
EPS = 1e-05
THETA = 500000.0
MASKED = -1e30
MESH = pl.DeviceIdType.MESH
BF16 = jnp.bfloat16
F32 = jnp.float32


def place():
    dp, tensor = lax.axis_index("dp"), lax.axis_index("tensor")
    return dp // 2, dp % 2, tensor // SIDE, tensor % SIDE


def device(x, core, z, y):
    return (2 * (x % SIDE) + core, SIDE * (z % SIDE) + y % SIDE)


def greet(others):
    barrier = pltpu.get_barrier_semaphore()
    for other in others:
        pl.semaphore_signal(barrier, inc=1, device_id=other, device_id_type=MESH)
    pl.semaphore_wait(barrier, len(others))


def remote(src, dst, send, recv, other):
    return pltpu.make_async_remote_copy(
        src_ref=src, dst_ref=dst, send_sem=send, recv_sem=recv, device_id=other, device_id_type=MESH
    )


def rotate(v, cos, sin):
    return v * cos + pltpu.roll(v, HEAD // 2, 1) * sin


def pieces(own, every, step, size, offset=0, cols=None):
    across = slice(None) if cols is None else pl.ds(*cols)

    def at(n):
        return pl.ds(pl.multiple_of(n * step + offset, size), size)

    return lambda n: own.at[at(n), across], lambda s, n: every.at[s, at(n), :]


class Spread:
    def __init__(self, own, block, bulk, send, recv):
        self.own, self.block, self.bulk, self.send, self.recv = own, block, bulk, send, recv
        self.x, self.core, self.z, self.y = place()

    def number(self, parity, core, half):
        return 4 * parity + 2 * core + half

    def up(self, n):
        return (self.x, self.core, self.z, self.y + n)

    def copy(self, i, d, piece, to, first=False):
        slot = (self.y + d + SIDE) % SIDE
        src = self.own(piece) if first else self.block(slot, piece)
        return remote(
            src, self.block(slot, piece), self.send, self.recv.at[min(i, 12)], device(*to)
        )

    def mine(self, half):
        return self.number(self.x % 2, self.core, half)

    def sends(self, i):
        if i in (0, 1):
            return self.copy(i, 0, self.mine(i), self.up(1), True)
        if i == 2:
            return self.copy(i, 3, self.mine(0), self.up(1))
        if i in (3, 4):
            return self.copy(i, 0, self.mine(4 - i), self.up(SIDE - 1), True)
        if i == 5:
            return self.copy(i, 1, self.mine(1), self.up(SIDE - 1))
        d, half = 1 + (i % 6) // 2, i % 2
        if i < 12:
            to = (self.x + (SIDE - 1 if half else 1), self.core, self.z, self.y)
            return self.copy(i, d, self.mine(half), to)
        parity = self.x % 2 if i < 18 else 1 - self.x % 2
        piece = self.number(parity, self.core, half)
        return self.copy(i, d, piece, (self.x, 1 - self.core, self.z, self.y))

    def got(self, i):
        if i < 6:
            d = {0: 3, 1: 3, 2: 2, 3: 1, 4: 1, 5: 2}[i]
            half = {0: 0, 1: 1, 2: 0, 3: 1, 4: 0, 5: 1}[i]
            piece = self.mine(half)
        else:
            d, half = 1 + (i % 6) // 2, i % 2
            piece = self.number(1 - self.x % 2, self.core, half)
        view = self.block((self.y + d) % SIDE, piece)
        remote(view, view, self.send, self.recv.at[i], device(*self.up(1))).wait_recv()

    def start(self):
        for i in (0, 3, 1, 4):
            self.sends(i).start()

    def along_y(self, i):
        self.got(i)
        if i == 0:
            self.sends(2).start()
        if i == 3:
            self.sends(5).start()
        d = {0: 3, 1: 3, 2: 2, 3: 1, 4: 1, 5: 2}[i]
        half = {0: 0, 1: 1, 2: 0, 3: 1, 4: 0, 5: 1}[i]
        self.sends(6 + 2 * (d - 1) + half).start()
        self.sends(12 + 2 * (d - 1) + half).start()

    def along_x(self, i):
        self.got(i)
        self.sends(i + 12).start()

    def sibling(self):
        view = self.bulk(1)
        remote(view, view, self.send, self.recv.at[12], device(*self.up(1))).wait_recv()

    def sent(self):
        view = self.bulk(2)
        remote(view, view, self.send, self.recv.at[12], device(*self.up(1))).wait_send()


Y_ROUNDS = ((0, 3), (1, 4), (2, 5))
X_ROUNDS = ((10, 7), (11, 6), (8, 9))
PIECE = 16


def spread_rows(row):
    return jnp.transpose(jnp.broadcast_to(row, (128, row.shape[1])))


def count(flags):
    return jnp.sum(jnp.where(flags, 1.0, 0.0), axis=0, keepdims=True)


def describe(seg_ids, seg_doc, doc_lens, y):
    lane = lax.broadcasted_iota(jnp.int32, (1, 128), 1)

    def window(n):
        return seg_ids[:, pl.ds(pl.multiple_of(128 * jnp.maximum(n, 0), 128), 128)].astype(F32)

    own = [window(SIDE * s + y) for s in range(SIDE)]
    own_at = [(128 * (SIDE * s + y) + lane).astype(F32) for s in range(SIDE)]
    halo, halo_at = [], []
    for s in (0, 2):
        low, high = window(SIDE * s + y - 1), window(SIDE * (s + 1) + y - 1)
        both = jnp.where(lane < HALO, pltpu.roll(low, HALO, 1), high)
        start = jnp.where(
            lane < HALO, 128 * (SIDE * s + y) - HALO, 128 * (SIDE * (s + 1) + y) - 2 * HALO
        )
        at = (start + lane).astype(F32)
        halo.append(jnp.where(at < 0.0, -1.0, both))
        halo_at.append(at)
    seg = jnp.concatenate(own + halo, axis=1)
    at = jnp.concatenate(own_at + halo_at, axis=1)
    keys = seg.shape[1]
    tokens = SIDE * 128
    number = lax.broadcasted_iota(jnp.int32, (128, keys), 0).astype(F32)
    docs = spread_rows(seg_doc[...].astype(F32))
    docs = jnp.concatenate([docs] * (keys // 128), axis=1)
    doc = jnp.sum(jnp.where(number == seg, docs, 0.0), axis=0, keepdims=True)
    order = jnp.where(seg < 0.0, 65536.0 + at, doc * 2048.0 + at)
    tall, tall_seg = spread_rows(order), spread_rows(seg)
    key_rank, rank, pos = [], [], []
    for c in range(keys // 128):
        cut = slice(128 * c, 128 * (c + 1))
        less = tall < order[:, cut]
        key_rank.append(count(less))
        if c < SIDE:
            rank.append(count(less[:tokens]))
            pos.append(count(less & (tall_seg == seg[:, cut])))
    key_rank, rank, pos = [jnp.concatenate(v, axis=1) for v in (key_rank, rank, pos)]
    doc = doc[:, :tokens]
    low, high = jnp.zeros_like(doc), jnp.zeros_like(doc)
    for d in range(doc_lens.shape[0]):
        length = doc_lens[d].astype(F32)
        low = low + jnp.where(doc > d, length, 0.0)
        high = high + jnp.where(doc >= d, length, 0.0)
    mine = key_rank[:, :tokens]
    ranges = [low, high, mine - pos, mine + 1.0]
    coarse = [jnp.floor(v * (1.0 / 64.0)) for v in ranges]
    fine = [v - 64.0 * c for v, c in zip(ranges, coarse)]
    table = jnp.concatenate(coarse + fine + [rank] * 8, axis=0)
    return table, jnp.concatenate([key_rank] * 8, axis=0), pos


def gather_project(
    gain_far, hid_far, seg_ids_far, seg_doc_far, doc_lens_far, wq, wkv, pfx, wo,
    q_out, kv, pfx_all, wo_low, table, key_table,
    xs, wqs, wkvs, cos, sin, gain, hid, seg_ids, seg_doc, doc_lens,
    send, recv, x_send, x_recv, halo_send, halo_recv, stay,
):
    x, core, z, y = place()
    here = lambda dx, dcore, dz, dy: device(
        x + dx, core if dcore == 0 else 1 - core, z + dz, y + dy
    )
    down = SIDE - 1
    stays = [
        pltpu.make_async_copy(src, dst, stay.at[k])
        for k, (src, dst) in enumerate(
            [
                (hid_far, hid),
                (gain_far, gain),
                (seg_ids_far, seg_ids),
                (seg_doc_far, seg_doc),
                (doc_lens_far, doc_lens),
                (wkv, wkvs.at[y]),
                (wq, wqs.at[y]),
                (pfx, pfx_all.at[y]),
                (wo.at[:, pl.ds(0, wo_low.shape[2])], wo_low.at[y]),
            ]
        )
    ]
    for copy in stays:
        copy.start()
    greet([
        here(0, 0, 0, 1), here(0, 0, 0, down), here(0, 0, 1, 0), here(0, 0, down, 0),
        here(1, 0, 0, 0), here(down, 0, 0, 0), here(0, 1, 0, 0),
    ])

    def third(array, size):
        return lambda n: array.at[pl.ds(0, 3), pl.ds(0, n * size), :]

    parts = [
        pieces(wkv, wkvs, 512, 512) + (third(wkvs, 2048),),
        pieces(wq, wqs, 512, 256) + (third(wqs, 1024),),
        pieces(wq, wqs, 512, 256, 256) + (third(wqs, 1024),),
        pieces(pfx, pfx_all, 512, 512) + (third(pfx_all, 2048),),
        pieces(wo, wo_low, 32, 32, 0, (0, wo_low.shape[2])) + (third(wo_low, 128),),
    ]
    units = [Spread(*part, send.at[k], recv.at[k]) for k, part in enumerate(parts)]
    units[0].start()

    stays[0].wait()
    stays[1].wait()
    values = hid[...].astype(F32)
    scale = lax.rsqrt(jnp.mean(values * values, axis=-1, keepdims=True) + EPS)
    wide = gain[...].astype(F32)
    wide = jnp.concatenate([wide[r : r + 1, :] for r in range(wide.shape[0])], axis=1)
    xs[z] = (values * scale * wide).astype(BF16)

    per_half = HALO // PIECE

    def x_copy(side, n, d=0):
        view = xs.at[(z + d) % SIDE, pl.ds(PIECE * n, PIECE), :]
        i = n + (2 * per_half if d else 0)
        to = here(0, 0, down if side else 1, 0)
        return remote(view, view, x_send.at[side], x_recv.at[side, i], to)

    def first_half(side, k):
        return (k + per_half * side) % (2 * per_half)

    def x_own(k):
        if k < 2 * per_half:
            for side in range(2):
                x_copy(side, first_half(side, k)).start()

    def x_got(k):
        for side in range(2):
            d = 1 if side else down
            if k < 2 * per_half:
                n = first_half(side, k)
                view = xs.at[(z + d) % SIDE, pl.ds(PIECE * n, PIECE), :]
                i = n
            else:
                n = first_half(side, k - 2 * per_half)
                view = xs.at[(z + 2) % SIDE, pl.ds(PIECE * n, PIECE), :]
                i = n + 2 * per_half
            remote(view, view, x_send.at[side], x_recv.at[side, i], here(0, 0, 1, 0)).wait_recv()
            if k < per_half:
                x_copy(side, n, d).start()

    tokens = SIDE * 128
    def both(ds):
        return jnp.concatenate([xs[(z + d) % SIDE] for d in ds], axis=0)

    def group(d):
        return pl.ds(pl.multiple_of((z + d) % SIDE * 128, 128), 128)

    def project_kv(ds):
        for h in range(2):
            weight = jnp.concatenate([wkvs[2 * h], wkvs[2 * h + 1]], axis=1)
            got = jnp.dot(both(ds), weight, preferred_element_type=F32)
            for n, d in enumerate(ds):
                part, at = got[128 * n : 128 * (n + 1)], group(d)
                key = rotate(part[:, :HEAD], cos[at, :], sin[at, :])
                kv[at, pl.ds(2 * HEAD * h, HEAD)] = key.astype(BF16)
                kv[at, pl.ds(2 * HEAD * h + HEAD, HEAD)] = part[:, HEAD:].astype(BF16)

    def project_q(ds, s):
        got = jnp.dot(both(ds), wqs[s], preferred_element_type=F32)
        for n, d in enumerate(ds):
            part, at = got[128 * n : 128 * (n + 1)], group(d)
            for m in range(2):
                one = rotate(part[:, HEAD * m : HEAD * (m + 1)], cos[at, :], sin[at, :])
                q_out[at, pl.ds(HEAD * (2 * s + m), HEAD)] = one.astype(BF16)

    def halo_copy(slot):
        dst = (slot + y // 3) % SIDE
        return remote(
            kv.at[pl.ds(128 * slot + HALO, HALO), :],
            kv.at[pl.ds(pl.multiple_of(tokens + HALO * dst, HALO), HALO), :],
            halo_send.at[slot],
            halo_recv.at[slot],
            here(0, 0, 0, 1),
        )

    def describe_tokens():
        for k in range(2, 5):
            stays[k].wait()
        rows, key_rows, pos = describe(seg_ids, seg_doc, doc_lens, y)
        table[...] = rows
        key_table[...] = key_rows
        cos[...] = spread_rows(pos)

    def rotary_tables():
        lane = lax.broadcasted_iota(jnp.int32, (1, HEAD), 1)
        inverse = jnp.zeros((1, HEAD), F32)
        for i in range(HEAD // 2):
            inverse = jnp.where(lane % (HEAD // 2) == i, THETA ** (-2.0 * i / HEAD), inverse)
        angle = (pfx.shape[0] + cos[...]) * inverse
        cos[...] = jnp.cos(angle)
        turn = jnp.sin(angle)
        sin[...] = jnp.where(lane < HEAD // 2, -turn, turn)

    early, late = (0, 1), (3, 2)

    def early_kv():
        stays[5].wait()
        units[0].sibling()
        project_kv(early)

    def early_q():
        stays[6].wait()
        for unit in units[1:3]:
            unit.sibling()
        project_q(early, 0)
        project_q(early, 1)

    def late_kv():
        project_kv(late)
        for slot in range(SIDE):
            halo_copy(slot).start()

    extra = {
        3: [describe_tokens],
        6: [rotary_tables],
        9: [early_kv],
        11: [early_q],
        12: [lambda: project_q(early, 2), lambda: project_q(early, 3)],
        13: [late_kv],
        14: [lambda: project_q(late, 0), lambda: project_q(late, 1)],
        15: [lambda: project_q(late, 2), lambda: project_q(late, 3)],
    }
    lag = 2
    ahead = 8
    for k in range(ahead):
        x_own(k)
    for t in range(max(3 * len(units) + lag, 18)):
        if t < 3 * len(units):
            for i in Y_ROUNDS[t % 3]:
                units[t // 3].along_y(i)
            if t % 3 == 0 and t // 3 + 1 < len(units):
                units[t // 3 + 1].start()
        if 1 <= t < 3 * per_half + 1:
            x_got(t - 1)
            x_own(t - 1 + ahead)
        if lag <= t < 3 * len(units) + lag:
            for i in X_ROUNDS[(t - lag) % 3]:
                units[(t - lag) // 3].along_x(i)
        for work in extra.get(t, []):
            work()
    for unit in units[3:]:
        unit.sibling()
    for k in range(7, 9):
        stays[k].wait()
    for slot in range(SIDE):
        halo_copy(slot).wait()
    for side in range(2):
        view = xs.at[pl.ds(0, 3), pl.ds(0, HALO), :]
        remote(view, view, x_send.at[side], x_recv.at[side, 0], here(0, 0, 1, 0)).wait_send()
    for unit in units:
        unit.sent()


TILE = 128
NEW_KEYS = 384
PREFIX_KEYS = 512


def attend(
    table, key_table, q, kv, pfx, out,
    perm, qs, kvs, ranges, outs, top, acc, new_scores, prefix_scores,
):
    tokens, news, prefix = q.shape[0], kv.shape[0], pfx.shape[1]
    group = 4
    exponent = math.log2(math.e) / math.sqrt(HEAD)

    def one_hot(flags):
        return jnp.where(flags, 1.0, 0.0).astype(BF16)

    rank = table[8:9, :]
    spots = lax.broadcasted_iota(jnp.int32, (tokens, tokens), 0).astype(F32)
    by_doc = one_hot(spots == rank)
    qs[...] = jnp.dot(by_doc, q[...], preferred_element_type=F32).astype(BF16)
    got = lax.dot_general(
        by_doc, table[...].astype(BF16), (((1,), (1,)), ((), ())), preferred_element_type=F32
    )
    for k in range(4):
        column = 64.0 * got[:, k : k + 1] + got[:, k + 4 : k + 5]
        ranges[k] = jnp.broadcast_to(column, (tokens, 128)).astype(jnp.int32)
    spots = lax.broadcasted_iota(jnp.int32, (news, news), 0).astype(F32)
    kvs[...] = jnp.dot(
        one_hot(spots == key_table[0:1, :]), kv[...], preferred_element_type=F32
    ).astype(BF16)
    tall = spread_rows(rank)
    lane = lax.broadcasted_iota(jnp.int32, (tokens, 128), 1)
    for c in range(tokens // 128):
        perm[:, pl.ds(128 * c, 128)] = one_hot(tall == (lane + 128 * c).astype(F32))

    @pl.loop(0, tokens // TILE)
    def _(i):
        cut = pl.ds(pl.multiple_of(i * TILE, TILE), TILE)
        top[...] = jnp.full(top.shape, MASKED, F32)
        acc[...] = jnp.zeros(acc.shape, F32)
        queries = [
            jnp.concatenate(
                [qs[cut, pl.ds(HEAD * (group * h + n), HEAD)] for n in range(group)], axis=0
            )
            for h in range(2)
        ]

        def extent(kind, keys):
            first = jnp.min(ranges[kind, cut, :]) // 128 * 128
            last = jnp.max(ranges[kind + 1, cut, :])
            return first, (last - first + keys - 1) // keys

        def begin_at(first, j, keys, size):
            return pl.multiple_of(jnp.minimum(first + j * keys, size - keys), 128)

        def score(kind, where, keys, size, load, scores):
            first, steps = where

            @pl.loop(0, steps)
            def _(j):
                start = begin_at(first, j, keys, size)
                near = jnp.maximum(ranges[kind, cut, :], first + j * keys) - start
                far = ranges[kind + 1, cut, :] - start
                at = lax.broadcasted_iota(jnp.int32, (TILE, 128), 1)
                bias = jnp.concatenate(
                    [
                        jnp.where((at + c >= near) & (at + c < far), 0.0, MASKED)
                        for c in range(0, keys, 128)
                    ],
                    axis=1,
                )
                bias = jnp.concatenate([bias] * group, axis=0)
                for h in range(2):
                    s = bias + lax.dot_general(
                        queries[h],
                        load(2 * h, pl.ds(start, keys)),
                        (((1,), (1,)), ((), ())),
                        preferred_element_type=F32,
                    )
                    scores[h, j] = s
                    best = top[h]
                    for c in range(0, keys, 128):
                        best = jnp.maximum(best, s[:, c : c + 128])
                    top[h] = best

        def weigh(where, keys, size, load, scores):
            first, steps = where

            @pl.loop(0, steps)
            def _(j):
                start = begin_at(first, j, keys, size)
                for h in range(2):
                    best = jnp.concatenate([top[h]] * (keys // 128), axis=1)
                    p = jnp.exp2((scores[h, j] - best) * exponent).astype(BF16)
                    value = load(2 * h + 1, pl.ds(start, keys))
                    value = jnp.concatenate([value, jnp.ones_like(value)], axis=1)
                    acc[h] += jnp.dot(p, value, preferred_element_type=F32)

        load_new = lambda column, at: kvs[at, pl.ds(HEAD * column, HEAD)]
        load_prefix = lambda column, at: pfx[column, at, :]
        own, doc = extent(2, NEW_KEYS), extent(0, PREFIX_KEYS)
        score(2, own, NEW_KEYS, news, load_new, new_scores)
        score(0, doc, PREFIX_KEYS, prefix, load_prefix, prefix_scores)
        for h in range(2):
            best = jnp.max(top[h], axis=1, keepdims=True)
            top[h] = jnp.broadcast_to(best, top.shape[1:])
        weigh(own, NEW_KEYS, news, load_new, new_scores)
        weigh(doc, PREFIX_KEYS, prefix, load_prefix, prefix_scores)
        for h in range(2):
            done = (acc[h, :, pl.ds(0, HEAD)] / acc[h, :, pl.ds(HEAD, HEAD)]).astype(BF16)
            for n in range(group):
                outs[cut, pl.ds(HEAD * (group * h + n), HEAD)] = done[n * TILE : (n + 1) * TILE]

    out[...] = jnp.dot(perm[...], outs[...], preferred_element_type=F32).astype(BF16)


COLS = 512


def project_reduce(
    att, wo_low, wo, hid_far, mixed,
    wo_high, hid, far_out, near_out, far_in, near_in,
    far_send, far_recv, near_send, near_recv, send, recv, stay,
):
    x, core, z, y = place()
    down = SIDE - 1
    sides = [device(x, core, z + 1, y), device(x, core, z + down, y)]
    half = wo_low.shape[2]
    stays = [
        pltpu.make_async_copy(wo.at[:, pl.ds(half, half)], wo_high.at[y], stay.at[0]),
        pltpu.make_async_copy(hid_far, hid, stay.at[1]),
    ]
    for copy in stays:
        copy.start()
    greet(
        sides
        + [device(x, core, z, y + 1), device(x, core, z, y + down)]
        + [device(x + 1, core, z, y), device(x + down, core, z, y), device(x, 1 - core, z, y)]
    )
    bulk = lambda n: wo_high.at[pl.ds(0, 3), pl.ds(0, 128 * n), :]
    unit = Spread(*pieces(wo, wo_high, 32, 32, 0, (half, half)), bulk, send.at[0], recv.at[0])
    unit.start()
    chunks = 2 * half // COLS

    def partial(slot, j):
        source, at = (wo_low, j) if j < chunks // 2 else (wo_high, j - chunks // 2)
        weight = source[:, :, pl.ds(COLS * at, COLS)].reshape(-1, COLS)
        return jnp.dot(att[slot % SIDE], weight, preferred_element_type=F32)

    def far(j):
        return remote(far_out.at[j], far_in.at[j], far_send.at[0], far_recv.at[j], sides[j % 2])

    def near(side, j):
        return remote(
            near_out.at[side, j],
            near_in.at[side, j],
            near_send.at[0],
            near_recv.at[side, j],
            sides[side],
        )

    def far_step(j):
        far_out[j] = partial(z + 2, j).astype(BF16)
        far(j).start()

    def near_step(j):
        side = 1 - j % 2
        near_out[side, j] = partial(z + (down if side else 1), j).astype(BF16)
        near(side, j).start()
        side = j % 2
        mine = partial(z + (down if side else 1), j)
        far(j).wait_recv()
        near_out[side, j] = (mine + far_in[j].astype(F32)).astype(BF16)
        near(side, j).start()

    def along_y(r):
        for i in Y_ROUNDS[r]:
            unit.along_y(i)

    def along_x(r):
        for i in X_ROUNDS[r]:
            unit.along_x(i)

    for j in range(chunks // 2):
        far_step(j)
    step = chunks // 8
    along_y(0)
    for j in range(2 * step):
        near_step(j)
    along_y(1)
    along_x(0)
    for j in range(2 * step, 3 * step):
        near_step(j)
    along_y(2)
    along_x(1)
    for j in range(3 * step, 4 * step):
        near_step(j)
    along_x(2)
    stays[0].wait()
    unit.sibling()
    for j in range(chunks // 2, chunks):
        far_step(j)
    for j in range(chunks // 2, chunks):
        near_step(j)
    stays[1].wait()
    for j in range(chunks):
        cut = pl.ds(COLS * j, COLS)
        mine = partial(z, j) + hid[:, cut].astype(F32)
        near(0, j).wait_recv()
        near(1, j).wait_recv()
        mine = mine + near_in[0, j].astype(F32) + near_in[1, j].astype(F32)
        mixed[:, cut] = mine.astype(BF16)
    remote(far_out, far_in, far_send.at[0], far_recv.at[0], sides[0]).wait_send()
    remote(near_out, near_in, near_send.at[0], near_recv.at[0, 0], sides[0]).wait_send()
    unit.sent()


def local(hidden_in, norm_gain, w_query, keyvalue_weight, w_out, cache, seg_ids, seg_doc, doc_lens):
    prefix_len = cache.shape[0]
    width = hidden_in.shape[1]
    half = width // 2
    far = lambda array: pltpu.with_memory_space_constraint(array, pltpu.HBM)
    vmem = pl.BlockSpec(memory_space=pltpu.VMEM)
    whole = pl.BlockSpec(memory_space=pltpu.HBM)
    tokens = SIDE * 128
    news = tokens + SIDE * HALO
    q, kv, pfx, wo_low, table, key_table = pl.pallas_call(
        gather_project,
        out_shape=(
            jax.ShapeDtypeStruct((tokens, 8 * HEAD), BF16),
            jax.ShapeDtypeStruct((news, 4 * HEAD), BF16),
            jax.ShapeDtypeStruct((SIDE, prefix_len, HEAD), BF16),
            jax.ShapeDtypeStruct((SIDE, w_out.shape[0], half), BF16),
            jax.ShapeDtypeStruct((16, tokens), F32),
            jax.ShapeDtypeStruct((8, news), F32),
        ),
        in_specs=[whole] * 9,
        out_specs=(vmem,) * 6,
        scratch_shapes=[
            pltpu.VMEM((SIDE, 128, width), BF16),
            pltpu.VMEM((SIDE,) + w_query.shape, BF16),
            pltpu.VMEM((SIDE,) + keyvalue_weight.shape, BF16),
            pltpu.VMEM((tokens, HEAD), F32),
            pltpu.VMEM((tokens, HEAD), F32),
            pltpu.VMEM((width // 128, 128), BF16),
            pltpu.VMEM(hidden_in.shape, BF16),
            pltpu.VMEM((1,) + seg_ids.shape, jnp.int32),
            pltpu.VMEM((1,) + seg_doc.shape, jnp.int32),
            pltpu.SMEM(doc_lens.shape, jnp.int32),
            pltpu.SemaphoreType.DMA((5,)),
            pltpu.SemaphoreType.DMA((5, 13)),
            pltpu.SemaphoreType.DMA((2,)),
            pltpu.SemaphoreType.DMA((2, 16)),
            pltpu.SemaphoreType.DMA((4,)),
            pltpu.SemaphoreType.DMA((4,)),
            pltpu.SemaphoreType.DMA((9,)),
        ],
        compiler_params=pltpu.CompilerParams(
            collective_id=0, has_side_effects=True, vmem_limit_bytes=30 * 2**20
        ),
        name="gather_project",
    )(
        far(norm_gain.reshape(-1, 128)),
        far(hidden_in),
        far(seg_ids[None, :]),
        far(seg_doc[None, :]),
        far(doc_lens),
        far(w_query),
        far(keyvalue_weight),
        far(cache),
        far(w_out),
    )

    attended = pl.pallas_call(
        attend,
        out_shape=jax.ShapeDtypeStruct((tokens, 8 * HEAD), BF16),
        in_specs=[vmem] * 5,
        out_specs=vmem,
        scratch_shapes=[
            pltpu.VMEM((tokens, tokens), BF16),
            pltpu.VMEM((tokens, 8 * HEAD), BF16),
            pltpu.VMEM((news, 4 * HEAD), BF16),
            pltpu.VMEM((4, tokens, 128), jnp.int32),
            pltpu.VMEM((tokens, 8 * HEAD), BF16),
            pltpu.VMEM((2, 4 * TILE, 128), F32),
            pltpu.VMEM((2, 4 * TILE, 2 * HEAD), F32),
            pltpu.VMEM((2, pl.cdiv(news, NEW_KEYS), 4 * TILE, NEW_KEYS), F32),
            pltpu.VMEM((2, prefix_len // PREFIX_KEYS, 4 * TILE, PREFIX_KEYS), F32),
        ],
        compiler_params=pltpu.CompilerParams(vmem_limit_bytes=40 * 2**20),
        name="attend",
    )(table, key_table, q, kv, pfx)

    chunks = width // COLS
    return pl.pallas_call(
        project_reduce,
        out_shape=jax.ShapeDtypeStruct(hidden_in.shape, BF16),
        in_specs=[vmem] * 2 + [whole] * 2,
        out_specs=vmem,
        scratch_shapes=[
            pltpu.VMEM((SIDE, w_out.shape[0], half), BF16),
            pltpu.VMEM(hidden_in.shape, BF16),
            pltpu.VMEM((chunks, 128, COLS), BF16),
            pltpu.VMEM((2, chunks, 128, COLS), BF16),
            pltpu.VMEM((chunks, 128, COLS), BF16),
            pltpu.VMEM((2, chunks, 128, COLS), BF16),
            pltpu.SemaphoreType.DMA((1,)),
            pltpu.SemaphoreType.DMA((chunks,)),
            pltpu.SemaphoreType.DMA((1,)),
            pltpu.SemaphoreType.DMA((2, chunks)),
            pltpu.SemaphoreType.DMA((1,)),
            pltpu.SemaphoreType.DMA((1, 13)),
            pltpu.SemaphoreType.DMA((2,)),
        ],
        compiler_params=pltpu.CompilerParams(
            collective_id=1, has_side_effects=True, vmem_limit_bytes=32 * 2**20
        ),
        name="project_reduce",
    )(attended.reshape(SIDE, 128, 8 * HEAD), wo_low, far(w_out), far(hidden_in))


def solution(mesh):
    return jax.shard_map(
        local,
        mesh=mesh,
        in_specs=(
            P(("dp", "tensor"), None),
            P(),
            P(None, "tensor"),
            P(None, "tensor"),
            P("tensor", None),
            P(None, "tensor"),
            P("dp"),
            P("dp"),
            P(),
        ),
        out_specs=P(("dp", "tensor"), None),
        check_vma=False,
    )
```
